32 devices in a mesh: dp: 16 (over z, y, core), pipe: 2 (over x).
Axes of the slice: x: 2, y: 2, z: 4, core: 2. Of those that a mesh axis runs over, the one named last changes fastest.
Arguments:
- master: float32 [2, 2, 8192, 256], P('pipe', None, 'dp'), may hold values from -12 to 12
- grads: float32 [2, 2, 8192, 256], P('pipe', None, 'dp'), may hold values from -60 to 60
- first_moment: float32 [2, 2, 8192, 256], P('pipe', None, 'dp'), may hold values from -4 to 4
- second_moment: float32 [2, 2, 8192, 256], P('pipe', None, 'dp'), may hold values from 0.05 to 2
- tokens: bfloat16 [2, 2688, 8192], P('pipe', 'dp'), may hold values from -20 to 20
Outputs:
- new_master: float32 [2, 2, 8192, 256], P('pipe', None, 'dp')
- new_first: float32 [2, 2, 8192, 256], P('pipe', None, 'dp')
- new_second: float32 [2, 2, 8192, 256], P('pipe', None, 'dp')
- passed: bfloat16 [2, 2688, 1024], P('pipe', 'dp')
The draws below stay inside these ranges and needn't reach their ends.
All inputs are finite; a program needn't handle non-finite values.
Results may differ from the reference program's by a relative error of at most 0.012.
The reference program's roundings to bfloat16 on the way count: a program that leaves them out, or rounds other values in their place, can miss the bound.
Values may be sent and summed in bfloat16 or wider, within the bound.
A program may use at most 64 MiB of HBM per device.

```python
import math
import jax
import jax.numpy as jnp
from jax import lax

D = 8192
HEAD = 128
QH = 8
BLOCKS = 2
STEP = 10
SEQ = 168
KVW = 256
N_DP = 16
N_PIPE = 2


def draw_master(key, part):
    base = jax.random.normal(key, (N_PIPE, BLOCKS, D, 2 * HEAD), jnp.float32) * D ** (-0.5)
    return base


def draw_grads(key, part):
    base = jax.random.normal(key, (N_PIPE, BLOCKS, D, 2 * HEAD), jnp.float32)
    base = jnp.clip(base, -5.0, 5.0)
    rows = jnp.arange(D).astype(jnp.float32)
    rise = 1.0 + 2.0 * rows / (D - 1)
    base = base * rise[None, None, :, None]
    return base


def draw_tokens(key, part):
    shape = (N_PIPE, SEQ * N_DP, D)
    base = jnp.clip(jax.random.normal(key, shape, jnp.float32), -6.0, 6.0)
    return base.astype(jnp.bfloat16)


def shard_levels(rng, dims, pieces, least, high):
    level = 1.0
    for axis_at, blocks in pieces:
        heights = jax.random.uniform(jax.random.fold_in(jax.random.fold_in(rng, 6), axis_at), (blocks,), jnp.float32, least / len(pieces), high / len(pieces))
        level = level * jnp.repeat(jnp.exp(heights), dims[axis_at] // blocks).reshape((-1,) + (1,) * (len(dims) - 1 - axis_at))
    return level


def bell_draw(stream_key, shape, spread, bound, cuts=(), held_as=jnp.bfloat16):
    values = jax.random.normal(stream_key, shape, jnp.float32) * spread
    if len(cuts) > 0:
        values = shard_levels(stream_key, shape, cuts, -0.22, 0.18) * values
    return jnp.clip(values, min=-bound, max=bound).astype(held_as)


def setup_inputs(seed: int = 0) -> dict:
    seeds = jax.random.split(jax.random.key(seed), 6)
    return {
        "master": draw_master(jax.random.fold_in(seeds[5], 71), 0),
        "grads": draw_grads(jax.random.fold_in(seeds[5], 71), 0),
        "first_moment": bell_draw(seeds[2], (N_PIPE, BLOCKS, D, KVW), 0.5, 4.0, ((0, 2), (2, 16)), jnp.float32),
        "second_moment": jnp.clip(jnp.exp(math.log(2.0) - 3.6888794 * jax.random.uniform(seeds[3], (N_PIPE, BLOCKS, D, KVW), jnp.float32) ** shard_levels(seeds[3], (N_PIPE, BLOCKS, D, KVW), ((0, 2), (2, 16)), -0.2, 0.2)), 0.05, 2.0),
        "tokens": draw_tokens(jax.random.fold_in(seeds[5], 71), 0),
    }


def attend(xseq, weight):
    xf = xseq.astype(jnp.float32)
    mean_sq = lax.optimization_barrier(jnp.mean(xf * xf, axis=1, keepdims=True))
    normed = (xf * lax.rsqrt(mean_sq + 1e-06)).astype(jnp.bfloat16)
    kv_proj = jnp.dot(normed, weight, preferred_element_type=jnp.float32)
    keys = kv_proj[:, :HEAD].astype(jnp.bfloat16)
    values = kv_proj[:, HEAD:].astype(jnp.bfloat16)
    rows = xseq.shape[0]
    queries = normed[:, :QH * HEAD].reshape(rows, QH, HEAD).astype(jnp.float32)
    scores = jnp.einsum('shd,td->hst', queries, keys.astype(jnp.float32)) / jnp.sqrt(jnp.float32(HEAD))
    causal = jnp.arange(rows)[:, None] >= jnp.arange(rows)[None, :]
    scores = jnp.where(causal[None], scores, -1e+30)
    top = lax.optimization_barrier(jnp.max(scores, axis=2, keepdims=True))
    expd = jnp.exp(scores - top)
    probs = (expd / lax.optimization_barrier(jnp.sum(expd, axis=2, keepdims=True))).astype(jnp.bfloat16)
    attn = jnp.einsum('hst,td->shd', probs.astype(jnp.float32), values.astype(jnp.float32)).reshape(rows, QH * HEAD)
    return (xf[:, :QH * HEAD] + attn).astype(jnp.bfloat16)

def reference(master, grads, first_moment, second_moment, tokens):
    square_sum = jnp.sum(grads * grads)
    count = jnp.float32(grads.size)
    clip = jnp.minimum(1.0, 0.5 * jnp.sqrt(count) / jnp.sqrt(square_sum + 1e-06))
    scaled = clip * grads
    new_first = 0.9 * first_moment + 0.1 * scaled
    new_second = 0.95 * second_moment + 0.05 * scaled * scaled
    step_mean = new_first / (1.0 - 0.9 ** STEP)
    step_var = new_second / (1.0 - 0.95 ** STEP)
    new_master = master - 0.003 * step_mean / (jnp.sqrt(step_var) + 1e-08)
    outputs = []
    for section in range(N_PIPE):
        weight = new_master[section, 0].astype(jnp.bfloat16)
        seqs = tokens[section].reshape(N_DP, SEQ, D)
        result = lax.map(lambda s: attend(s, weight), seqs)
        outputs.append(result.reshape(N_DP * SEQ, QH * HEAD))
    stacked = jnp.stack(outputs, axis=0)
    passed = jnp.roll(stacked, 1, axis=0)
    return (new_master, new_first, new_second, passed)
```

```python
import functools
import math

import jax
import jax.numpy as jnp
import numpy as np
from jax import lax
from jax.experimental import pallas as pl
from jax.experimental.pallas import tpu as pltpu
from jax.sharding import PartitionSpec as P

HEAD = 128
QH = 8
PIECE = 256
TURNED = 0
CHUNK = 128
PAIR_TURNED = 1
STEP = 10
WIDTH = QH * HEAD
MESH = pl.DeviceIdType.MESH


def adam(master, grads, first_moment, second_moment, clip):
    scaled = clip * grads
    new_first = 0.9 * first_moment + 0.1 * scaled
    new_second = 0.95 * second_moment + 0.05 * scaled * scaled
    step_mean = new_first / (1.0 - 0.9**STEP)
    step_var = new_second / (1.0 - 0.95**STEP)
    new_master = master - 0.003 * step_mean / (jnp.sqrt(step_var) + 1e-08)
    return new_master, new_first, new_second


def kernel(
    n_dp, n_pipe, count, turned,
    master, grads, first, second, tokens,
    new_master, new_first, new_second, passed,
    g_v, m_v, f_v, s_v, x_v, n_v, w, acc, part, slots, inv, kv, q_n,
    far_x, far_inv, far_kv,
    load_sem, own_sem, part_send, part_recv, z_send, y_send, c_send, w_recv,
    far_send, far_recv,
):
    me = lax.axis_index("dp")
    sec = lax.axis_index("pipe")
    total = n_dp * n_pipe
    lines, cores = 2, 2
    depth = n_dp // (lines * cores)
    core = lax.rem(me, cores)
    line = lax.rem(lax.div(me, cores), lines)
    z = lax.div(me, lines * cores)
    mine = (z, line, core)
    rows = g_v.shape[1]
    pieces = w_recv.shape[1]
    piece = rows // pieces
    dim = x_v.shape[1]
    seq = x_v.shape[0]

    def at(zz, yy, cc):
        return (zz * lines + yy) * cores + cc

    blocks = g_v.shape[0]
    states = ((master, m_v), (first, f_v), (second, s_v))
    loads = [
        pltpu.make_async_copy(grads.at[0], g_v, load_sem.at[0]),
        *[
            pltpu.make_async_copy(src.at[0, 0], dst.at[0], load_sem.at[1 + i])
            for i, (src, dst) in enumerate(states)
        ],
        pltpu.make_async_copy(tokens.at[0], x_v, load_sem.at[4]),
        *[
            pltpu.make_async_copy(
                src.at[0, pl.ds(1, blocks - 1)], dst.at[pl.ds(1, blocks - 1)], load_sem.at[5 + i]
            )
            for i, (src, dst) in enumerate(states)
        ],
    ]
    loads[0].start()

    flat = sec * n_dp + me

    def peer(k):
        other = lax.rem(flat + k, total)
        return {"dp": lax.rem(other, n_dp), "pipe": lax.div(other, n_dp)}

    barrier = pltpu.get_barrier_semaphore()

    @pl.loop(1, total)
    def _(k):
        pl.semaphore_signal(barrier, inc=1, device_id=peer(k), device_id_type=MESH)

    for load in loads[1:]:
        load.start()

    loads[0].wait()
    cols = g_v.shape[2]
    local = jnp.zeros((8, cols), jnp.float32)
    for b in range(blocks):
        g = g_v[b]
        local = local + jnp.sum((g * g).reshape(rows // 8, 8, cols), axis=0)
    lanes = local[:, :128]
    for i in range(1, cols // 128):
        lanes = lanes + local[:, i * 128 : (i + 1) * 128]
    part[...] = jnp.sum(lanes, axis=0, keepdims=True)

    pl.semaphore_wait(barrier, total - 1)

    own = pltpu.make_async_copy(part, slots.at[flat], part_recv)
    own.start()

    @pl.loop(1, total)
    def _(k):
        pltpu.make_async_remote_copy(
            src_ref=part, dst_ref=slots.at[flat], send_sem=part_send, recv_sem=part_recv,
            device_id=peer(k), device_id_type=MESH,
        ).start()

    after = lax.rem(sec + 1, n_pipe)

    def to_next(src, dst, i):
        return pltpu.make_async_remote_copy(
            src_ref=src, dst_ref=dst, send_sem=far_send.at[i], recv_sem=far_recv.at[i],
            device_id={"dp": me, "pipe": after}, device_id_type=MESH,
        )

    head_copy = to_next(tokens.at[0, :, pl.ds(0, WIDTH)], far_x, 0)

    loads[4].wait()
    step = 512

    def squares(i, carry):
        for j in range(step // 128):
            x = x_v[:, pl.ds(pl.multiple_of(i * step + j * 128, 128), 128)].astype(jnp.float32)
            carry = carry + x * x
        return carry

    sq = lax.fori_loop(0, dim // step, squares, jnp.zeros((seq, 128), jnp.float32))
    mean_sq = jnp.sum(sq, axis=1, keepdims=True) / dim
    inv[...] = jnp.broadcast_to(lax.rsqrt(mean_sq + 1e-06), (seq, 128))
    inv_copy = to_next(inv, far_inv, 1)
    inv_copy.start()

    @pl.loop(0, dim // step)
    def _(i):
        scale = inv[...]
        for j in range(step // 128):
            at_cols = pl.ds(pl.multiple_of(i * step + j * 128, 128), 128)
            n_v[:, at_cols] = (x_v[:, at_cols].astype(jnp.float32) * scale).astype(jnp.bfloat16)

    for load in loads[1:4]:
        load.wait()
    acc[...] = jnp.zeros_like(acc)

    pltpu.make_async_copy(slots, slots, part_recv).wait()
    summed = jnp.sum(slots[...], axis=0)
    square_sum = jnp.sum(summed, axis=1, keepdims=True)
    root = np.float32(0.5) * np.sqrt(np.float32(count))
    clip = jnp.minimum(1.0, root / jnp.sqrt(square_sum + 1e-06))

    def span(b, ch):
        return pl.ds(pl.multiple_of(at(*b) * rows + ch * piece, piece), piece)

    def send(b, ch, dst, sem):
        return pltpu.make_async_remote_copy(
            src_ref=w.at[span(b, ch)], dst_ref=w.at[span(b, ch)],
            send_sem=sem, recv_sem=w_recv.at[at(*b), ch],
            device_id={"dp": dst, "pipe": sec}, device_id_type=MESH,
        )

    def chip(b):
        return b[0]

    def up(b, ch, other=0):
        return send(b, ch, at(z + 1, line, core), z_send.at[0, other, chip(b), ch])

    def down(b, ch, other=0):
        return send(b, ch, at(z - 1, line, core), z_send.at[1, other, chip(b), ch])

    def across(b, ch):
        return send(b, ch, at(z, 1 - line, core), y_send.at[chip(b), ch])

    def beside(b, ch):
        return send(b, ch, at(z, line, 1 - core), c_send.at[b[0] * lines + b[1], ch])

    def arrived(b, ch):
        send(b, ch, me, c_send.at[0, 0]).wait_recv()

    def both_ways(b, ch, other=0):
        @pl.when(z < depth - 1)
        def _():
            up(b, ch, other).start()

        @pl.when(z > 0)
        def _():
            down(b, ch, other).start()

    whole_blocks = rows % 128 == 0

    def multiply(b):
        if whole_blocks:
            at_rows = pl.ds(pl.multiple_of(at(*b) * rows, rows), rows)
            acc[...] += jnp.dot(n_v[:, at_rows], w[at_rows, :], preferred_element_type=jnp.float32)

    def update(b, r):
        results = adam(m_v[b, r, :], g_v[b, r, :], f_v[b, r, :], s_v[b, r, :], clip)
        for ref, result in zip((new_master, new_first, new_second), results):
            ref[0, b, r, :] = result
        return results[0]

    def multiply_piece(b, ch):
        if whole_blocks:
            at_rows = span(b, ch)
            acc[...] += jnp.dot(n_v[:, at_rows], w[at_rows, :], preferred_element_type=jnp.float32)

    for ch in range(pieces):
        w[span(mine, ch), :] = update(0, pl.ds(ch * piece, piece)).astype(jnp.bfloat16)
        both_ways(mine, ch)
        across(mine, ch).start()
        beside(mine, ch).start()

    head_copy.start()
    multiply(mine)

    for ch in range(turned):
        b = (z, 1 - line, core)
        arrived(b, ch)
        both_ways(b, ch, 1)
        beside(b, ch).start()

    for t in range(depth):
        far = t + 1
        if far < depth:
            for other in (0, 1):
                for ch in range(pieces if other == 0 else turned):

                    def along(zz, onward, end):
                        b = (zz, (line, 1 - line)[other], core)
                        arrived(b, ch)

                        @pl.when(end)
                        def _():
                            onward(b, ch, other).start()

                        if other == 0 and ch >= turned:
                            across(b, ch).start()
                        beside(b, ch).start()

                    @pl.when(z - far >= 0)
                    def _():
                        along(z - far, up, z < depth - 1)

                    @pl.when(z + far < depth)
                    def _():
                        along(z + far, down, z > 0)

        def at_distance(visit):
            if t == 0:
                visit(z)
            else:

                @pl.when(z - t >= 0)
                def _():
                    visit(z - t)

                @pl.when(z + t < depth)
                def _():
                    visit(z + t)

        last = t == depth - 1
        if last:

            def use_own(zz):
                multiply((zz, line, core))
                b = (zz, line, 1 - core)
                for ch in range(pieces):
                    arrived(b, ch)
                multiply(b)

            at_distance(use_own)
        for ch in range(turned, pieces):

            def pass_on(zz):
                b = (zz, 1 - line, core)
                arrived(b, ch)
                beside(b, ch).start()
                if last:
                    multiply_piece(b, ch)

            at_distance(pass_on)

        def use(zz):
            if last:
                for ch in range(turned):
                    multiply_piece((zz, 1 - line, core), ch)
                b = (zz, 1 - line, 1 - core)
                for ch in range(pieces):
                    arrived(b, ch)
                    multiply_piece(b, ch)
                return
            if t > 0:
                multiply((zz, line, core))
            multiply((zz, 1 - line, core))
            for yy in (line, 1 - line):
                b = (zz, yy, 1 - core)
                for ch in range(pieces):
                    arrived(b, ch)
                multiply(b)

        if t == 0:
            for load in loads[5:]:
                load.wait()
            for b in range(1, blocks):
                for ch in range(pieces):
                    update(b, pl.ds(ch * piece, piece))
        if t == min(2, depth - 1):
            head_copy.wait_recv()
            inv_copy.wait_recv()
            for h in range(QH):
                hs = pl.ds(h * HEAD, HEAD)
                q_n[:, hs] = (far_x[:, hs].astype(jnp.float32) * far_inv[...]).astype(jnp.bfloat16)
        at_distance(use)

    if whole_blocks:
        projected = acc[...]
    else:

        def run(i, carry):
            d = pl.ds(pl.multiple_of(i * step, step), step)
            return carry + jnp.dot(n_v[:, d], w[d, :], preferred_element_type=jnp.float32)

        projected = lax.fori_loop(0, dim // step, run, acc[...])
    kv[...] = projected.astype(jnp.bfloat16)
    kv_copy = to_next(kv, far_kv, 2)
    kv_copy.start()
    row = lax.broadcasted_iota(jnp.int32, (seq, seq), 0)
    col = lax.broadcasted_iota(jnp.int32, (seq, seq), 1)
    causal = row >= col
    kv_copy.wait_recv()
    keys = far_kv[:, :HEAD]
    values = far_kv[:, HEAD:]
    for h in range(QH):
        hs = pl.ds(h * HEAD, HEAD)
        scores = lax.dot_general(
            q_n[:, hs], keys, (((1,), (1,)), ((), ())), preferred_element_type=jnp.float32
        ) * np.float32(1.0 / math.sqrt(HEAD))
        scores = jnp.where(causal, scores, -1e30)
        top = jnp.max(scores, axis=1, keepdims=True)
        expd = jnp.exp(scores - top)
        probs = (expd / jnp.sum(expd, axis=1, keepdims=True)).astype(jnp.bfloat16)
        attn = jnp.dot(probs, values, preferred_element_type=jnp.float32)
        passed[0, :, hs] = (far_x[:, hs].astype(jnp.float32) + attn).astype(jnp.bfloat16)

    for c in (head_copy, inv_copy, kv_copy):
        c.wait_send()
    pltpu.make_async_copy(
        slots.at[pl.ds(0, total - 1)], slots.at[pl.ds(0, total - 1)], part_send
    ).wait()
    for ch in range(pieces):
        for zz in range(depth):
            for other in range(2 if ch < turned else 1):
                b = (zz, (line, 1 - line)[other], core)

                @pl.when(jnp.logical_and(zz <= z, z < depth - 1))
                def _():
                    up(b, ch, other).wait_send()

                @pl.when(jnp.logical_and(zz >= z, z > 0))
                def _():
                    down(b, ch, other).wait_send()

            b = (zz, line, core)
            if ch >= turned:
                across(b, ch).wait_send()
            else:

                @pl.when(zz == z)
                def _():
                    across(b, ch).wait_send()

            for yy in range(lines):
                beside((zz, yy, core), ch).wait_send()


def paired(
    n_dp, n_pipe, count, turned,
    master, grads, first, second, tokens,
    new_master, new_first, new_second, passed,
    g_v, m_v, f_v, s_v, x_v, n_v, w, acc_k, acc_v, part, slots, sums, inv, kv, q_n, probs,
    far_x, far_inv, far_kv,
    load_sem, part_send, part_recv, sum_send, sum_recv, ready, p_send, q_send, y_send, c_send,
    w_recv, far_send, far_recv,
):
    me = lax.axis_index("dp")
    sec = lax.axis_index("pipe")
    lines, cores, depth = 2, 2, 4
    group = n_pipe * lines * cores
    core = lax.rem(me, cores)
    line = lax.rem(lax.div(me, cores), lines)
    z = lax.div(me, lines * cores)
    seat = sec * lines * cores + lax.rem(me, lines * cores)
    upper = lax.div(z, 2)
    inner = jnp.logical_or(z == 1, z == 2)
    outer = jnp.logical_not(inner)
    planes = (z, 1 - z + 4 * upper, 2 - upper, 3 - 3 * upper)
    blocks, rows, cols = g_v.shape
    seq, dim = x_v.shape
    chunk = CHUNK
    chunks = rows // chunk
    units = [(h, c) for h in range(2) for c in range(chunks)]
    straight = [u for u in units if u[0] == 0 or u[1] >= turned]
    turns = [(1, c) for c in range(turned)]

    def at(zz, yy, cc):
        return (zz * lines + yy) * cores + cc

    def device(zz, r):
        return {"dp": zz * lines * cores + lax.rem(r, lines * cores), "pipe": lax.div(r, lines * cores)}

    states = ((master, m_v), (first, f_v), (second, s_v))
    loads = [
        pltpu.make_async_copy(grads.at[0], g_v, load_sem.at[0]),
        *[
            pltpu.make_async_copy(src.at[0, 0], dst.at[0], load_sem.at[1 + i])
            for i, (src, dst) in enumerate(states)
        ],
        pltpu.make_async_copy(tokens.at[0], x_v, load_sem.at[4]),
        *[
            pltpu.make_async_copy(
                src.at[0, pl.ds(1, blocks - 1)], dst.at[pl.ds(1, blocks - 1)], load_sem.at[5 + i]
            )
            for i, (src, dst) in enumerate(states)
        ],
    ]
    loads[0].start()
    barrier = pltpu.get_barrier_semaphore()

    @pl.loop(1, group)
    def _(k):
        pl.semaphore_signal(
            barrier, inc=1, device_id=device(z, lax.rem(seat + k, group)), device_id_type=MESH
        )

    @pl.loop(0, group * (depth - 1 - z))
    def _(k):
        pl.semaphore_signal(
            barrier, inc=1, device_id=device(z + 1 + lax.div(k, group), lax.rem(k, group)),
            device_id_type=MESH,
        )

    loads[4].start()
    for load in loads[1:4] + loads[5:]:
        load.start()

    for k in range(depth):

        @pl.when(z == k)
        def _():
            pl.semaphore_wait(barrier, group - 1 + group * k)

    @pl.loop(0, z)
    def _(zz):
        pl.semaphore_signal(
            ready.at[z], inc=1, device_id=device(zz, seat), device_id_type=MESH
        )

    loads[0].wait()
    local = jnp.zeros((8, cols), jnp.float32)
    for b in range(blocks):
        g = g_v[b]
        local = local + jnp.sum((g * g).reshape(rows // 8, 8, cols), axis=0)
    lanes = local[:, :128]
    for i in range(1, cols // 128):
        lanes = lanes + local[:, i * 128 : (i + 1) * 128]
    part[...] = jnp.sum(lanes, axis=0, keepdims=True)


    def give(zz, r):
        return pltpu.make_async_remote_copy(
            src_ref=part, dst_ref=slots.at[z * group + seat], send_sem=part_send,
            recv_sem=part_recv.at[z], device_id=device(zz, r), device_id_type=MESH,
        )

    own = pltpu.make_async_copy(part, slots.at[z * group + seat], part_recv.at[z])
    own.start()

    @pl.loop(0, group * z)
    def _(k):
        give(lax.div(k, group), lax.rem(k, group)).start()

    @pl.loop(1, group)
    def _(k):
        give(z, lax.rem(seat + k, group)).start()

    after = lax.rem(sec + 1, n_pipe)

    def to_next(src, dst, i):
        return pltpu.make_async_remote_copy(
            src_ref=src, dst_ref=dst, send_sem=far_send.at[i], recv_sem=far_recv.at[i],
            device_id={"dp": me, "pipe": after}, device_id_type=MESH,
        )

    head_copy = to_next(tokens.at[0, :, pl.ds(0, WIDTH)], far_x, 0)

    loads[4].wait()
    step = 512

    def squares(i, carry):
        for j in range(step // 128):
            x = x_v[:, pl.ds(pl.multiple_of(i * step + j * 128, 128), 128)].astype(jnp.float32)
            carry = carry + x * x
        return carry

    sq = lax.fori_loop(0, dim // step, squares, jnp.zeros((seq, 128), jnp.float32))
    mean_sq = jnp.sum(sq, axis=1, keepdims=True) / dim
    inv[...] = jnp.broadcast_to(lax.rsqrt(mean_sq + 1e-06), (seq, 128))
    inv_copy = to_next(inv, far_inv, 1)


    @pl.loop(0, dim // step)
    def _(i):
        scale = inv[...]
        for j in range(step // 128):
            at_cols = pl.ds(pl.multiple_of(i * step + j * 128, 128), 128)
            n_v[:, at_cols] = (x_v[:, at_cols].astype(jnp.float32) * scale).astype(jnp.bfloat16)

    acc_k[...] = jnp.zeros_like(acc_k)
    acc_v[...] = jnp.zeros_like(acc_v)

    def plane_slots(zz):
        return slots.at[pl.ds(zz * group, group)]

    def plane_wait(zz):
        pltpu.make_async_copy(plane_slots(zz), plane_slots(zz), part_recv.at[zz]).wait()

    plane_wait(z)
    sums[z] = jnp.sum(plane_slots(z)[...], axis=0)

    def lift(zz):
        return pltpu.make_async_remote_copy(
            src_ref=sums.at[z], dst_ref=sums.at[z], send_sem=sum_send.at[zz],
            recv_sem=sum_recv.at[z], device_id=device(zz, seat), device_id_type=MESH,
        )

    for zz in range(1, depth):

        @pl.when(z < zz)
        def _():
            pl.semaphore_wait(ready.at[zz], 1)
            lift(zz).start()

    for load in loads[1:4]:
        load.wait()
    for zz in range(depth):

        @pl.when(zz > z)
        def _():
            plane_wait(zz)
            sums[zz] = jnp.sum(plane_slots(zz)[...], axis=0)

        @pl.when(zz < z)
        def _():
            pltpu.make_async_copy(sums.at[zz], sums.at[zz], sum_recv.at[zz]).wait()

    square_sum = jnp.sum(jnp.sum(sums[...], axis=0), axis=1, keepdims=True)
    root = np.float32(0.5) * np.sqrt(np.float32(count))
    clip = jnp.minimum(1.0, root / jnp.sqrt(square_sum + 1e-06))

    def send(b, u, dst, sem):
        h, c = u
        here = w.at[h, pl.ds(pl.multiple_of(at(*b) * rows + c * chunk, chunk), chunk)]
        return pltpu.make_async_remote_copy(
            src_ref=here, dst_ref=here, send_sem=sem, recv_sem=w_recv.at[h, at(*b), c],
            device_id={"dp": dst, "pipe": sec}, device_id_type=MESH,
        )

    beyond = jnp.where(z == 1, 2, 1)

    def to_pair(b, u):
        send(b, u, at(planes[1], line, core), p_send).start()

    def to_beyond(b, u):
        send(b, u, at(beyond, line, core), q_send).start()

    def across(b, u):
        send(b, u, at(z, 1 - line, core), y_send).start()

    def beside(b, u):
        send(b, u, at(z, line, 1 - core), c_send).start()

    def arrived(b, u):
        send(b, u, me, c_send).wait_recv()

    def here(s):
        return (planes[s], line, core)

    def there(s):
        return (planes[s], 1 - line, core)

    def update(b, r, hs):
        results = adam(m_v[b, r, hs], g_v[b, r, hs], f_v[b, r, hs], s_v[b, r, hs], clip)
        for ref, result in zip((new_master, new_first, new_second), results):
            ref[0, b, r, hs] = result
        return results[0]

    def product(h, zz, yy, cc, low=0, high=None):
        size = (rows if high is None else high) - low
        d = pl.ds(pl.multiple_of(at(zz, yy, cc) * rows + low, 128), size)
        acc = (acc_k, acc_v)[h]
        acc[...] += jnp.dot(n_v[:, d], w[h, d, :], preferred_element_type=jnp.float32)

    def multiply(s, h):
        @pl.loop(0, cores)
        def _(cc):
            product(h, planes[s], line, cc)
            product(h, planes[s], 1 - line, cc, turned * chunk if h and s else 0)

    def from_beside(s, own_units, other_units):
        for u in own_units:
            arrived((planes[s], line, 1 - core), u)
        for u in other_units:
            arrived((planes[s], 1 - line, 1 - core), u)

    for h, c in units:
        r = pl.ds(c * chunk, chunk)
        w[h, pl.ds(pl.multiple_of(me * rows + c * chunk, chunk), chunk), :] = update(
            0, r, slice(h * HEAD, (h + 1) * HEAD)
        ).astype(jnp.bfloat16)
        u = (h, c)
        to_pair(here(0), u)

        @pl.when(inner)
        def _():
            to_beyond(here(0), u)

        across(here(0), u)
        beside(here(0), u)

    head_copy.start()
    inv_copy.start()
    for load in loads[5:]:
        load.wait()
    for b in range(1, blocks):
        for c in range(chunks):
            for h in range(2):
                update(b, pl.ds(c * chunk, chunk), slice(h * HEAD, (h + 1) * HEAD))

    for u in units:
        arrived(here(1), u)

        @pl.when(inner)
        def _():
            to_beyond(here(1), u)
            arrived(here(2), u)
            to_pair(here(2), u)
            beside(here(2), u)

        if u in straight:
            across(here(1), u)
        beside(here(1), u)
        arrived(there(0), u)
        beside(there(0), u)

    @pl.when(inner)
    def _():
        for u in straight:
            across(here(2), u)
        for u in turns:
            to_beyond(there(0), u)

    @pl.when(outer)
    def _():
        for u in turns:
            to_pair(there(0), u)

    from_beside(0, units, units)
    multiply(0, 0)
    multiply(0, 1)

    for u in units:

        @pl.when(inner)
        def _():
            arrived(here(3), u)
            to_pair(here(3), u)
            across(here(3), u) if u in straight else None
            beside(here(3), u)

        @pl.when(outer)
        def _():
            arrived(here(2), u)
            across(here(2), u) if u in straight else None
            beside(here(2), u)

        if u in straight:
            arrived(there(1), u)
            beside(there(1), u)

    @pl.when(inner)
    def _():
        for u in turns:
            arrived(there(1), u)
            to_beyond(there(1), u)
            beside(there(1), u)
            to_pair(there(0), u)
        for s in (2, 3):
            for u in turns:
                arrived(there(s), u)
                to_pair(there(s), u)
                beside(there(s), u)

    from_beside(1, units, straight)
    multiply(1, 0)
    multiply(1, 1)
    head_copy.wait_recv()
    inv_copy.wait_recv()
    for h in range(QH):
        hs = pl.ds(h * HEAD, HEAD)
        q_n[:, hs] = (far_x[:, hs].astype(jnp.float32) * far_inv[...]).astype(jnp.bfloat16)

    for u in units:

        @pl.when(outer)
        def _():
            arrived(here(3), u)
            across(here(3), u) if u in straight else None
            beside(here(3), u)

        if u in straight:
            arrived(there(2), u)
            beside(there(2), u)

    from_beside(2, units, straight)
    multiply(2, 0)
    multiply(2, 1)

    for u in straight:
        if u[0] == 0:
            arrived(there(3), u)
            beside(there(3), u)
    from_beside(3, [u for u in units if u[0] == 0], [u for u in straight if u[0] == 0])
    multiply(3, 0)
    kv[0] = acc_k[...].astype(jnp.bfloat16)
    k_copy = to_next(kv.at[0], far_kv.at[0], 2)
    k_copy.start()
    for u in units:
        if u[0] == 1:
            arrived((planes[3], line, 1 - core), u)
    for cc in range(cores):
        product(1, planes[3], line, cc)
    last = [u for u in straight if u[0] == 1]
    for u in last:
        arrived(there(3), u)
        beside(there(3), u)

    @pl.when(outer)
    def _():
        for s in (1, 2, 3):
            for u in turns:
                arrived(there(s), u)
                beside(there(s), u)

    for u in last:
        arrived((planes[3], 1 - line, 1 - core), u)

    @pl.loop(0, cores)
    def _(cc):
        product(1, planes[3], 1 - line, cc, turned * chunk)

    if turned:
        for s in (1, 2, 3):
            for u in turns:
                arrived((planes[s], 1 - line, 1 - core), u)
        for s in (1, 2, 3):

            @pl.loop(0, cores)
            def _(cc):
                product(1, planes[s], 1 - line, cc, 0, turned * chunk)

    kv[1] = acc_v[...].astype(jnp.bfloat16)
    v_copy = to_next(kv.at[1], far_kv.at[1], 3)
    v_copy.start()
    row = lax.broadcasted_iota(jnp.int32, (seq, seq), 0)
    col = lax.broadcasted_iota(jnp.int32, (seq, seq), 1)
    causal = row >= col
    k_copy.wait_recv()
    keys = far_kv[0]
    for h in range(QH):
        hs = pl.ds(h * HEAD, HEAD)
        scores = lax.dot_general(
            q_n[:, hs], keys, (((1,), (1,)), ((), ())), preferred_element_type=jnp.float32
        ) * np.float32(1.0 / math.sqrt(HEAD))
        scores = jnp.where(causal, scores, -1e30)
        top = jnp.max(scores, axis=1, keepdims=True)
        expd = jnp.exp(scores - top)
        probs[h] = (expd / jnp.sum(expd, axis=1, keepdims=True)).astype(jnp.bfloat16)
    v_copy.wait_recv()
    values = far_kv[1]
    for h in range(QH):
        hs = pl.ds(h * HEAD, HEAD)
        attn = jnp.dot(probs[h], values, preferred_element_type=jnp.float32)
        passed[0, :, hs] = (far_x[:, hs].astype(jnp.float32) + attn).astype(jnp.bfloat16)

    for c in (head_copy, inv_copy, k_copy, v_copy):
        c.wait_send()

    for k in range(depth):

        @pl.when(z == k)
        def _():
            sent = slots.at[pl.ds(0, group - 1 + group * k)]
            pltpu.make_async_copy(sent, sent, part_send).wait()

    for zz in range(1, depth):

        @pl.when(z < zz)
        def _():
            lift(zz).wait_send()

    def sent(n, sem):
        span = w.at[0, pl.ds(0, n * chunk)]
        pltpu.make_async_copy(span, span, sem).wait()

    n, t = len(units), len(turns)

    @pl.when(inner)
    def _():
        sent(3 * (n + t), p_send)
        sent(2 * (n + t), q_send)

    @pl.when(outer)
    def _():
        sent(n + t, p_send)

    sent(n + 3 * len(straight), y_send)
    sent(8 * n, c_send)


def write_out(*refs):
    half = (len(refs) - 1) // 2
    sems = refs[-1]
    copies = [
        pltpu.make_async_copy(refs[i], refs[half + i], sems.at[i]) for i in range(half)
    ]
    for c in copies:
        c.start()
    for c in copies:
        c.wait()


def on_device(n_dp, n_pipe, master, grads, first_moment, second_moment, tokens):
    _, blocks, rows, cols = master.shape
    _, seq, dim = tokens.shape
    total = n_dp * n_pipe
    count = grads.size * total
    pieces = max(1, rows // PIECE)
    f32, bf16 = jnp.float32, jnp.bfloat16
    hbm = pl.BlockSpec(memory_space=pltpu.HBM)
    vmem = pl.BlockSpec(memory_space=pltpu.VMEM)
    dma = pltpu.SemaphoreType.DMA
    shapes = (
        *[jax.ShapeDtypeStruct(master.shape, f32)] * 3,
        jax.ShapeDtypeStruct((1, seq, WIDTH), bf16),
    )
    master, grads, first_moment, second_moment, tokens = (
        pltpu.with_memory_space_constraint(v, pltpu.HBM)
        for v in (master, grads, first_moment, second_moment, tokens)
    )
    depth = n_dp // 4
    if depth == 4 and rows % CHUNK == 0 and cols == 2 * HEAD:
        turned = PAIR_TURNED if rows // CHUNK > PAIR_TURNED else 0
        body = functools.partial(paired, n_dp, n_pipe, count, turned)
        scratch = [
            *[pltpu.VMEM((blocks, rows, cols), f32)] * 4,
            pltpu.VMEM((seq, dim), bf16),
            pltpu.VMEM((seq, dim), bf16),
            pltpu.VMEM((2, n_dp * rows, HEAD), bf16),
            pltpu.VMEM((seq, HEAD), f32),
            pltpu.VMEM((seq, HEAD), f32),
            pltpu.VMEM((1, 128), f32),
            pltpu.VMEM((total, 1, 128), f32),
            pltpu.VMEM((depth, 1, 128), f32),
            pltpu.VMEM((seq, 128), f32),
            pltpu.VMEM((2, seq, HEAD), bf16),
            pltpu.VMEM((seq, WIDTH), bf16),
            pltpu.VMEM((QH, seq, seq), bf16),
            pltpu.VMEM((seq, WIDTH), bf16),
            pltpu.VMEM((seq, 128), f32),
            pltpu.VMEM((2, seq, HEAD), bf16),
            dma((8,)),
            dma,
            dma((depth,)),
            dma((depth,)),
            dma((depth,)),
            pltpu.SemaphoreType.REGULAR((depth,)),
            dma,
            dma,
            dma,
            dma,
            dma((2, n_dp, rows // CHUNK)),
            dma((4,)),
            dma((4,)),
        ]
    else:
        body = functools.partial(kernel, n_dp, n_pipe, count, TURNED if pieces > TURNED else 0)
        scratch = [
            pltpu.VMEM((blocks, rows, cols), f32),
            pltpu.VMEM((blocks, rows, cols), f32),
            pltpu.VMEM((blocks, rows, cols), f32),
            pltpu.VMEM((blocks, rows, cols), f32),
            pltpu.VMEM((seq, dim), bf16),
            pltpu.VMEM((seq, dim), bf16),
            pltpu.VMEM((n_dp * rows, cols), bf16),
            pltpu.VMEM((seq, cols), f32),
            pltpu.VMEM((1, 128), f32),
            pltpu.VMEM((total, 1, 128), f32),
            pltpu.VMEM((seq, 128), f32),
            pltpu.VMEM((seq, cols), bf16),
            pltpu.VMEM((seq, WIDTH), bf16),
            pltpu.VMEM((seq, WIDTH), bf16),
            pltpu.VMEM((seq, 128), f32),
            pltpu.VMEM((seq, cols), bf16),
            dma((8,)),
            dma,
            dma,
            dma,
            dma((2, 2, depth, pieces)),
            dma((depth, pieces)),
            dma((n_dp // 2, pieces)),
            dma((n_dp, pieces)),
            dma((3,)),
            dma((3,)),
        ]
    results = pl.pallas_call(
        body,
        out_shape=tuple(pltpu.VMEM(v.shape, v.dtype) for v in shapes),
        in_specs=[hbm] * 5,
        out_specs=(vmem,) * 4,
        scratch_shapes=scratch,
        compiler_params=pltpu.CompilerParams(
            collective_id=0, has_side_effects=True, vmem_limit_bytes=48 * 1024 * 1024
        ),
        name="section",
    )(master, grads, first_moment, second_moment, tokens)
    return pl.pallas_call(
        write_out,
        out_shape=shapes,
        in_specs=[vmem] * 4,
        out_specs=(hbm,) * 4,
        scratch_shapes=[dma((4,))],
        compiler_params=pltpu.CompilerParams(vmem_limit_bytes=1024 * 1024),
        name="write_out",
    )(*results)


def solution(mesh):
    split = P("pipe", None, "dp", None)
    rows = P("pipe", "dp", None)
    return jax.shard_map(
        functools.partial(on_device, mesh.shape["dp"], mesh.shape["pipe"]),
        mesh=mesh,
        in_specs=(split, split, split, split, rows),
        out_specs=(split, split, split, rows),
        check_vma=False,
    )
```

```python
import functools
import math

import jax
import jax.numpy as jnp
import numpy as np
from jax import lax
from jax.experimental import pallas as pl
from jax.experimental.pallas import tpu as pltpu
from jax.sharding import PartitionSpec as P

HEAD = 128
QH = 8
PIECE = 256
TURNED = 0
CHUNK = 128
PAIR_TURNED = 1
STEP = 10
WIDTH = QH * HEAD
MESH = pl.DeviceIdType.MESH


def adam(master, grads, first_moment, second_moment, clip):
    scaled = clip * grads
    new_first = 0.9 * first_moment + 0.1 * scaled
    new_second = 0.95 * second_moment + 0.05 * scaled * scaled
    step_mean = new_first / (1.0 - 0.9**STEP)
    step_var = new_second / (1.0 - 0.95**STEP)
    new_master = master - 0.003 * step_mean / (jnp.sqrt(step_var) + 1e-08)
    return new_master, new_first, new_second


def kernel(
    n_dp, n_pipe, count, turned,
    master, grads, first, second, tokens,
    new_master, new_first, new_second, passed,
    g_v, m_v, f_v, s_v, x_v, n_v, w, acc, part, slots, inv, kv, q_n,
    far_x, far_inv, far_kv,
    load_sem, own_sem, part_send, part_recv, z_send, y_send, c_send, w_recv,
    far_send, far_recv,
):
    me = lax.axis_index("dp")
    sec = lax.axis_index("pipe")
    total = n_dp * n_pipe
    lines, cores = 2, 2
    depth = n_dp // (lines * cores)
    core = lax.rem(me, cores)
    line = lax.rem(lax.div(me, cores), lines)
    z = lax.div(me, lines * cores)
    mine = (z, line, core)
    rows = g_v.shape[1]
    pieces = w_recv.shape[1]
    piece = rows // pieces
    dim = x_v.shape[1]
    seq = x_v.shape[0]

    def at(zz, yy, cc):
        return (zz * lines + yy) * cores + cc

    blocks = g_v.shape[0]
    states = ((master, m_v), (first, f_v), (second, s_v))
    loads = [
        pltpu.make_async_copy(grads.at[0], g_v, load_sem.at[0]),
        *[
            pltpu.make_async_copy(src.at[0, 0], dst.at[0], load_sem.at[1 + i])
            for i, (src, dst) in enumerate(states)
        ],
        pltpu.make_async_copy(tokens.at[0], x_v, load_sem.at[4]),
        *[
            pltpu.make_async_copy(
                src.at[0, pl.ds(1, blocks - 1)], dst.at[pl.ds(1, blocks - 1)], load_sem.at[5 + i]
            )
            for i, (src, dst) in enumerate(states)
        ],
    ]
    loads[0].start()

    flat = sec * n_dp + me

    def peer(k):
        other = lax.rem(flat + k, total)
        return {"dp": lax.rem(other, n_dp), "pipe": lax.div(other, n_dp)}

    barrier = pltpu.get_barrier_semaphore()

    @pl.loop(1, total)
    def _(k):
        pl.semaphore_signal(barrier, inc=1, device_id=peer(k), device_id_type=MESH)

    for load in loads[1:]:
        load.start()

    loads[0].wait()
    cols = g_v.shape[2]
    local = jnp.zeros((8, cols), jnp.float32)
    for b in range(blocks):
        g = g_v[b]
        local = local + jnp.sum((g * g).reshape(rows // 8, 8, cols), axis=0)
    lanes = local[:, :128]
    for i in range(1, cols // 128):
        lanes = lanes + local[:, i * 128 : (i + 1) * 128]
    part[...] = jnp.sum(lanes, axis=0, keepdims=True)

    pl.semaphore_wait(barrier, total - 1)

    own = pltpu.make_async_copy(part, slots.at[flat], part_recv)
    own.start()

    @pl.loop(1, total)
    def _(k):
        pltpu.make_async_remote_copy(
            src_ref=part, dst_ref=slots.at[flat], send_sem=part_send, recv_sem=part_recv,
            device_id=peer(k), device_id_type=MESH,
        ).start()

    after = lax.rem(sec + 1, n_pipe)

    def to_next(src, dst, i):
        return pltpu.make_async_remote_copy(
            src_ref=src, dst_ref=dst, send_sem=far_send.at[i], recv_sem=far_recv.at[i],
            device_id={"dp": me, "pipe": after}, device_id_type=MESH,
        )

    head_copy = to_next(tokens.at[0, :, pl.ds(0, WIDTH)], far_x, 0)

    loads[4].wait()
    step = 512

    def squares(i, carry):
        for j in range(step // 128):
            x = x_v[:, pl.ds(pl.multiple_of(i * step + j * 128, 128), 128)].astype(jnp.float32)
            carry = carry + x * x
        return carry

    sq = lax.fori_loop(0, dim // step, squares, jnp.zeros((seq, 128), jnp.float32))
    mean_sq = jnp.sum(sq, axis=1, keepdims=True) / dim
    inv[...] = jnp.broadcast_to(lax.rsqrt(mean_sq + 1e-06), (seq, 128))
    inv_copy = to_next(inv, far_inv, 1)
    inv_copy.start()

    @pl.loop(0, dim // step)
    def _(i):
        scale = inv[...]
        for j in range(step // 128):
            at_cols = pl.ds(pl.multiple_of(i * step + j * 128, 128), 128)
            n_v[:, at_cols] = (x_v[:, at_cols].astype(jnp.float32) * scale).astype(jnp.bfloat16)

    for load in loads[1:4]:
        load.wait()
    acc[...] = jnp.zeros_like(acc)

    pltpu.make_async_copy(slots, slots, part_recv).wait()
    summed = jnp.sum(slots[...], axis=0)
    square_sum = jnp.sum(summed, axis=1, keepdims=True)
    root = np.float32(0.5) * np.sqrt(np.float32(count))
    clip = jnp.minimum(1.0, root / jnp.sqrt(square_sum + 1e-06))

    def span(b, ch):
        return pl.ds(pl.multiple_of(at(*b) * rows + ch * piece, piece), piece)

    def send(b, ch, dst, sem):
        return pltpu.make_async_remote_copy(
            src_ref=w.at[span(b, ch)], dst_ref=w.at[span(b, ch)],
            send_sem=sem, recv_sem=w_recv.at[at(*b), ch],
            device_id={"dp": dst, "pipe": sec}, device_id_type=MESH,
        )

    def chip(b):
        return b[0]

    def up(b, ch, other=0):
        return send(b, ch, at(z + 1, line, core), z_send.at[0, other, chip(b), ch])

    def down(b, ch, other=0):
        return send(b, ch, at(z - 1, line, core), z_send.at[1, other, chip(b), ch])

    def across(b, ch):
        return send(b, ch, at(z, 1 - line, core), y_send.at[chip(b), ch])

    def beside(b, ch):
        return send(b, ch, at(z, line, 1 - core), c_send.at[b[0] * lines + b[1], ch])

    def arrived(b, ch):
        send(b, ch, me, c_send.at[0, 0]).wait_recv()

    def both_ways(b, ch, other=0):
        @pl.when(z < depth - 1)
        def _():
            up(b, ch, other).start()

        @pl.when(z > 0)
        def _():
            down(b, ch, other).start()

    whole_blocks = rows % 128 == 0

    def multiply(b):
        if whole_blocks:
            at_rows = pl.ds(pl.multiple_of(at(*b) * rows, rows), rows)
            acc[...] += jnp.dot(n_v[:, at_rows], w[at_rows, :], preferred_element_type=jnp.float32)

    def update(b, r):
        results = adam(m_v[b, r, :], g_v[b, r, :], f_v[b, r, :], s_v[b, r, :], clip)
        for ref, result in zip((new_master, new_first, new_second), results):
            ref[0, b, r, :] = result
        return results[0]

    def multiply_piece(b, ch):
        if whole_blocks:
            at_rows = span(b, ch)
            acc[...] += jnp.dot(n_v[:, at_rows], w[at_rows, :], preferred_element_type=jnp.float32)

    for ch in range(pieces):
        w[span(mine, ch), :] = update(0, pl.ds(ch * piece, piece)).astype(jnp.bfloat16)
        both_ways(mine, ch)
        across(mine, ch).start()
        beside(mine, ch).start()

    head_copy.start()
    multiply(mine)

    for ch in range(turned):
        b = (z, 1 - line, core)
        arrived(b, ch)
        both_ways(b, ch, 1)
        beside(b, ch).start()

    for t in range(depth):
        far = t + 1
        if far < depth:
            for other in (0, 1):
                for ch in range(pieces if other == 0 else turned):

                    def along(zz, onward, end):
                        b = (zz, (line, 1 - line)[other], core)
                        arrived(b, ch)

                        @pl.when(end)
                        def _():
                            onward(b, ch, other).start()

                        if other == 0 and ch >= turned:
                            across(b, ch).start()
                        beside(b, ch).start()

                    @pl.when(z - far >= 0)
                    def _():
                        along(z - far, up, z < depth - 1)

                    @pl.when(z + far < depth)
                    def _():
                        along(z + far, down, z > 0)

        def at_distance(visit):
            if t == 0:
                visit(z)
            else:

                @pl.when(z - t >= 0)
                def _():
                    visit(z - t)

                @pl.when(z + t < depth)
                def _():
                    visit(z + t)

        last = t == depth - 1
        if last:

            def use_own(zz):
                multiply((zz, line, core))
                b = (zz, line, 1 - core)
                for ch in range(pieces):
                    arrived(b, ch)
                multiply(b)

            at_distance(use_own)
        for ch in range(turned, pieces):

            def pass_on(zz):
                b = (zz, 1 - line, core)
                arrived(b, ch)
                beside(b, ch).start()
                if last:
                    multiply_piece(b, ch)

            at_distance(pass_on)

        def use(zz):
            if last:
                for ch in range(turned):
                    multiply_piece((zz, 1 - line, core), ch)
                b = (zz, 1 - line, 1 - core)
                for ch in range(pieces):
                    arrived(b, ch)
                    multiply_piece(b, ch)
                return
            if t > 0:
                multiply((zz, line, core))
            multiply((zz, 1 - line, core))
            for yy in (line, 1 - line):
                b = (zz, yy, 1 - core)
                for ch in range(pieces):
                    arrived(b, ch)
                multiply(b)

        if t == 0:
            for load in loads[5:]:
                load.wait()
            for b in range(1, blocks):
                for ch in range(pieces):
                    update(b, pl.ds(ch * piece, piece))
        if t == min(2, depth - 1):
            head_copy.wait_recv()
            inv_copy.wait_recv()
            for h in range(QH):
                hs = pl.ds(h * HEAD, HEAD)
                q_n[:, hs] = (far_x[:, hs].astype(jnp.float32) * far_inv[...]).astype(jnp.bfloat16)
        at_distance(use)

    if whole_blocks:
        projected = acc[...]
    else:

        def run(i, carry):
            d = pl.ds(pl.multiple_of(i * step, step), step)
            return carry + jnp.dot(n_v[:, d], w[d, :], preferred_element_type=jnp.float32)

        projected = lax.fori_loop(0, dim // step, run, acc[...])
    kv[...] = projected.astype(jnp.bfloat16)
    kv_copy = to_next(kv, far_kv, 2)
    kv_copy.start()
    row = lax.broadcasted_iota(jnp.int32, (seq, seq), 0)
    col = lax.broadcasted_iota(jnp.int32, (seq, seq), 1)
    causal = row >= col
    kv_copy.wait_recv()
    keys = far_kv[:, :HEAD]
    values = far_kv[:, HEAD:]
    for h in range(QH):
        hs = pl.ds(h * HEAD, HEAD)
        scores = lax.dot_general(
            q_n[:, hs], keys, (((1,), (1,)), ((), ())), preferred_element_type=jnp.float32
        ) * np.float32(1.0 / math.sqrt(HEAD))
        scores = jnp.where(causal, scores, -1e30)
        top = jnp.max(scores, axis=1, keepdims=True)
        expd = jnp.exp(scores - top)
        probs = (expd / jnp.sum(expd, axis=1, keepdims=True)).astype(jnp.bfloat16)
        attn = jnp.dot(probs, values, preferred_element_type=jnp.float32)
        passed[0, :, hs] = (far_x[:, hs].astype(jnp.float32) + attn).astype(jnp.bfloat16)

    for c in (head_copy, inv_copy, kv_copy):
        c.wait_send()
    pltpu.make_async_copy(
        slots.at[pl.ds(0, total - 1)], slots.at[pl.ds(0, total - 1)], part_send
    ).wait()
    for ch in range(pieces):
        for zz in range(depth):
            for other in range(2 if ch < turned else 1):
                b = (zz, (line, 1 - line)[other], core)

                @pl.when(jnp.logical_and(zz <= z, z < depth - 1))
                def _():
                    up(b, ch, other).wait_send()

                @pl.when(jnp.logical_and(zz >= z, z > 0))
                def _():
                    down(b, ch, other).wait_send()

            b = (zz, line, core)
            if ch >= turned:
                across(b, ch).wait_send()
            else:

                @pl.when(zz == z)
                def _():
                    across(b, ch).wait_send()

            for yy in range(lines):
                beside((zz, yy, core), ch).wait_send()


def paired(
    n_dp, n_pipe, count, turned,
    master, grads, first, second, tokens,
    new_master, new_first, new_second, passed,
    g_v, m_v, f_v, s_v, x_v, n_v, w, acc, part, slots, sums, inv, kv, q_n, probs,
    far_x, far_inv, far_kv,
    load_sem, part_send, part_recv, sum_send, sum_recv, ready, p_send, q_send, y_send, c_send,
    w_recv, far_send, far_recv,
):
    me = lax.axis_index("dp")
    sec = lax.axis_index("pipe")
    lines, cores, depth = 2, 2, 4
    group = n_pipe * lines * cores
    core = lax.rem(me, cores)
    line = lax.rem(lax.div(me, cores), lines)
    z = lax.div(me, lines * cores)
    seat = sec * lines * cores + lax.rem(me, lines * cores)
    upper = lax.div(z, 2)
    inner = jnp.logical_or(z == 1, z == 2)
    outer = jnp.logical_not(inner)
    planes = (z, 1 - z + 4 * upper, 2 - upper, 3 - 3 * upper)
    blocks, rows, cols = g_v.shape
    seq, dim = x_v.shape
    chunk = CHUNK
    chunks = rows // chunk
    units = [(h, c) for h in range(2) for c in range(chunks)]
    straight = [u for u in units if u[0] == 0 or u[1] >= turned]
    turns = [(1, c) for c in range(turned)]

    def at(zz, yy, cc):
        return (zz * lines + yy) * cores + cc

    def device(zz, r):
        return {"dp": zz * lines * cores + lax.rem(r, lines * cores), "pipe": lax.div(r, lines * cores)}

    states = ((master, m_v), (first, f_v), (second, s_v))
    loads = [
        pltpu.make_async_copy(grads.at[0], g_v, load_sem.at[0]),
        *[
            pltpu.make_async_copy(src.at[0, 0], dst.at[0], load_sem.at[1 + i])
            for i, (src, dst) in enumerate(states)
        ],
        pltpu.make_async_copy(tokens.at[0], x_v, load_sem.at[4]),
        *[
            pltpu.make_async_copy(
                src.at[0, pl.ds(1, blocks - 1)], dst.at[pl.ds(1, blocks - 1)], load_sem.at[5 + i]
            )
            for i, (src, dst) in enumerate(states)
        ],
    ]
    loads[0].start()
    barrier = pltpu.get_barrier_semaphore()

    @pl.loop(1, group)
    def _(k):
        pl.semaphore_signal(
            barrier, inc=1, device_id=device(z, lax.rem(seat + k, group)), device_id_type=MESH
        )

    @pl.loop(0, group * (depth - 1 - z))
    def _(k):
        pl.semaphore_signal(
            barrier, inc=1, device_id=device(z + 1 + lax.div(k, group), lax.rem(k, group)),
            device_id_type=MESH,
        )

    loads[4].start()
    for load in loads[1:4] + loads[5:]:
        load.start()

    for k in range(depth):

        @pl.when(z == k)
        def _():
            pl.semaphore_wait(barrier, group - 1 + group * k)

    @pl.loop(0, z)
    def _(zz):
        pl.semaphore_signal(
            ready.at[z], inc=1, device_id=device(zz, seat), device_id_type=MESH
        )

    loads[0].wait()
    local = jnp.zeros((8, cols), jnp.float32)
    for b in range(blocks):
        g = g_v[b]
        local = local + jnp.sum((g * g).reshape(rows // 8, 8, cols), axis=0)
    lanes = local[:, :128]
    for i in range(1, cols // 128):
        lanes = lanes + local[:, i * 128 : (i + 1) * 128]
    part[...] = jnp.sum(lanes, axis=0, keepdims=True)


    def give(zz, r):
        return pltpu.make_async_remote_copy(
            src_ref=part, dst_ref=slots.at[z * group + seat], send_sem=part_send,
            recv_sem=part_recv.at[z], device_id=device(zz, r), device_id_type=MESH,
        )

    own = pltpu.make_async_copy(part, slots.at[z * group + seat], part_recv.at[z])
    own.start()

    @pl.loop(0, group * z)
    def _(k):
        give(lax.div(k, group), lax.rem(k, group)).start()

    @pl.loop(1, group)
    def _(k):
        give(z, lax.rem(seat + k, group)).start()

    after = lax.rem(sec + 1, n_pipe)

    def to_next(src, dst, i):
        return pltpu.make_async_remote_copy(
            src_ref=src, dst_ref=dst, send_sem=far_send.at[i], recv_sem=far_recv.at[i],
            device_id={"dp": me, "pipe": after}, device_id_type=MESH,
        )

    head_copy = to_next(tokens.at[0, :, pl.ds(0, WIDTH)], far_x, 0)

    loads[4].wait()
    step = 512

    def squares(i, carry):
        for j in range(step // 128):
            x = x_v[:, pl.ds(pl.multiple_of(i * step + j * 128, 128), 128)].astype(jnp.float32)
            carry = carry + x * x
        return carry

    sq = lax.fori_loop(0, dim // step, squares, jnp.zeros((seq, 128), jnp.float32))
    mean_sq = jnp.sum(sq, axis=1, keepdims=True) / dim
    inv[...] = jnp.broadcast_to(lax.rsqrt(mean_sq + 1e-06), (seq, 128))
    inv_copy = to_next(inv, far_inv, 1)


    @pl.loop(0, dim // step)
    def _(i):
        scale = inv[...]
        for j in range(step // 128):
            at_cols = pl.ds(pl.multiple_of(i * step + j * 128, 128), 128)
            n_v[:, at_cols] = (x_v[:, at_cols].astype(jnp.float32) * scale).astype(jnp.bfloat16)

    acc[...] = jnp.zeros_like(acc)

    def plane_slots(zz):
        return slots.at[pl.ds(zz * group, group)]

    def plane_wait(zz):
        pltpu.make_async_copy(plane_slots(zz), plane_slots(zz), part_recv.at[zz]).wait()

    plane_wait(z)
    sums[z] = jnp.sum(plane_slots(z)[...], axis=0)

    def lift(zz):
        return pltpu.make_async_remote_copy(
            src_ref=sums.at[z], dst_ref=sums.at[z], send_sem=sum_send.at[zz],
            recv_sem=sum_recv.at[z], device_id=device(zz, seat), device_id_type=MESH,
        )

    for zz in range(1, depth):

        @pl.when(z < zz)
        def _():
            pl.semaphore_wait(ready.at[zz], 1)
            lift(zz).start()

    for load in loads[1:4]:
        load.wait()
    for zz in range(depth):

        @pl.when(zz > z)
        def _():
            plane_wait(zz)
            sums[zz] = jnp.sum(plane_slots(zz)[...], axis=0)

        @pl.when(zz < z)
        def _():
            pltpu.make_async_copy(sums.at[zz], sums.at[zz], sum_recv.at[zz]).wait()

    square_sum = jnp.sum(jnp.sum(sums[...], axis=0), axis=1, keepdims=True)
    root = np.float32(0.5) * np.sqrt(np.float32(count))
    clip = jnp.minimum(1.0, root / jnp.sqrt(square_sum + 1e-06))

    def send(b, u, dst, sem):
        h, c = u
        here = w.at[h, pl.ds(pl.multiple_of(at(*b) * rows + c * chunk, chunk), chunk)]
        return pltpu.make_async_remote_copy(
            src_ref=here, dst_ref=here, send_sem=sem, recv_sem=w_recv.at[h, at(*b), c],
            device_id={"dp": dst, "pipe": sec}, device_id_type=MESH,
        )

    beyond = jnp.where(z == 1, 2, 1)

    def to_pair(b, u):
        send(b, u, at(planes[1], line, core), p_send).start()

    def to_beyond(b, u):
        send(b, u, at(beyond, line, core), q_send).start()

    def across(b, u):
        send(b, u, at(z, 1 - line, core), y_send).start()

    def beside(b, u):
        send(b, u, at(z, line, 1 - core), c_send).start()

    def arrived(b, u):
        send(b, u, me, c_send).wait_recv()

    def here(s):
        return (planes[s], line, core)

    def there(s):
        return (planes[s], 1 - line, core)

    def update(b, r, hs):
        results = adam(m_v[b, r, hs], g_v[b, r, hs], f_v[b, r, hs], s_v[b, r, hs], clip)
        for ref, result in zip((new_master, new_first, new_second), results):
            ref[0, b, r, hs] = result
        return results[0]

    halves = (slice(0, HEAD), slice(HEAD, 2 * HEAD))

    def product(h, s, yy, cc, low, size):
        d = pl.ds(pl.multiple_of(at(planes[s], yy, cc) * rows + low, 128), size)
        return jnp.dot(n_v[:, d], w[h, d, :], preferred_element_type=jnp.float32)

    def product_line(s, yy, h=None):
        d = pl.ds(pl.multiple_of(at(planes[s], yy, 0) * rows, rows), cores * rows)
        own = w[h, d, :] if h is not None else jnp.concatenate([w[0, d, :], w[1, d, :]], axis=1)
        return jnp.dot(n_v[:, d], own, preferred_element_type=jnp.float32)

    def straight_values(s):
        low = turned * chunk
        return product(1, s, 1 - line, 0, low, rows - low) + product(1, s, 1 - line, 1, low, rows - low)

    def multiply(s):
        acc[...] += product_line(s, line)
        acc[:, halves[0]] += product_line(s, 1 - line, 0)
        acc[:, halves[1]] += straight_values(s)

    def from_beside(s, own_units, other_units):
        for u in own_units:
            arrived((planes[s], line, 1 - core), u)
        for u in other_units:
            arrived((planes[s], 1 - line, 1 - core), u)

    for h, c in units:
        r = pl.ds(c * chunk, chunk)
        w[h, pl.ds(pl.multiple_of(me * rows + c * chunk, chunk), chunk), :] = update(
            0, r, slice(h * HEAD, (h + 1) * HEAD)
        ).astype(jnp.bfloat16)
        u = (h, c)
        to_pair(here(0), u)

        @pl.when(inner)
        def _():
            to_beyond(here(0), u)

        across(here(0), u)
        beside(here(0), u)

    head_copy.start()
    inv_copy.start()
    for load in loads[5:]:
        load.wait()
    for b in range(1, blocks):
        for c in range(chunks):
            for h in range(2):
                update(b, pl.ds(c * chunk, chunk), slice(h * HEAD, (h + 1) * HEAD))

    for u in units:
        arrived(here(1), u)

        @pl.when(inner)
        def _():
            to_beyond(here(1), u)
            arrived(here(2), u)
            to_pair(here(2), u)
            beside(here(2), u)

        if u in straight:
            across(here(1), u)
        beside(here(1), u)
        arrived(there(0), u)
        beside(there(0), u)

    @pl.when(inner)
    def _():
        for u in straight:
            across(here(2), u)
        for u in turns:
            to_beyond(there(0), u)

    @pl.when(outer)
    def _():
        for u in turns:
            to_pair(there(0), u)

    from_beside(0, units, units)
    acc[...] += product_line(0, line) + product_line(0, 1 - line)

    for u in units:

        @pl.when(inner)
        def _():
            arrived(here(3), u)
            to_pair(here(3), u)
            across(here(3), u) if u in straight else None
            beside(here(3), u)

        @pl.when(outer)
        def _():
            arrived(here(2), u)
            across(here(2), u) if u in straight else None
            beside(here(2), u)

        if u in straight:
            arrived(there(1), u)
            beside(there(1), u)

    @pl.when(inner)
    def _():
        for u in turns:
            arrived(there(1), u)
            to_beyond(there(1), u)
            beside(there(1), u)
            to_pair(there(0), u)
        for s in (2, 3):
            for u in turns:
                arrived(there(s), u)
                to_pair(there(s), u)
                beside(there(s), u)

    from_beside(1, units, straight)
    multiply(1)
    head_copy.wait_recv()
    inv_copy.wait_recv()
    for h in range(QH):
        hs = pl.ds(h * HEAD, HEAD)
        q_n[:, hs] = (far_x[:, hs].astype(jnp.float32) * far_inv[...]).astype(jnp.bfloat16)

    for u in units:

        @pl.when(outer)
        def _():
            arrived(here(3), u)
            across(here(3), u) if u in straight else None
            beside(here(3), u)

        if u in straight:
            arrived(there(2), u)
            beside(there(2), u)

    from_beside(2, units, straight)
    multiply(2)

    from_beside(3, [u for u in units if u[0] == 0], [])
    acc[:, halves[0]] += product_line(3, line, 0)
    for u in straight:
        if u[0] == 0:
            arrived(there(3), u)
            beside(there(3), u)
    from_beside(3, [], [u for u in units if u[0] == 0])
    kv[0] = (acc[:, halves[0]] + product_line(3, 1 - line, 0)).astype(jnp.bfloat16)
    k_copy = to_next(kv.at[0], far_kv.at[0], 2)
    k_copy.start()
    from_beside(3, [u for u in units if u[0] == 1], [])
    acc[:, halves[1]] += product_line(3, line, 1)
    last = [u for u in straight if u[0] == 1]

    def turns_here():
        @pl.when(outer)
        def _():
            for s in (1, 2, 3):
                for u in turns:
                    arrived(there(s), u)
                    beside(there(s), u)

    for u in last[:-1]:
        arrived(there(3), u)
        beside(there(3), u)
    turns_here()
    arrived(there(3), last[-1])
    beside(there(3), last[-1])
    if turned:
        for s in (1, 2, 3):
            for u in turns:
                arrived((planes[s], 1 - line, 1 - core), u)
        acc[:, halves[1]] += sum(
            product(1, s, 1 - line, cc, 0, turned * chunk) for s in (1, 2, 3) for cc in range(cores)
        )
    for u in last:
        arrived((planes[3], 1 - line, 1 - core), u)
    kv[1] = (acc[:, halves[1]] + straight_values(3)).astype(jnp.bfloat16)
    v_copy = to_next(kv.at[1], far_kv.at[1], 3)
    v_copy.start()
    row = lax.broadcasted_iota(jnp.int32, (seq, seq), 0)
    col = lax.broadcasted_iota(jnp.int32, (seq, seq), 1)
    causal = row >= col
    k_copy.wait_recv()
    keys = far_kv[0]
    for h in range(QH):
        hs = pl.ds(h * HEAD, HEAD)
        scores = lax.dot_general(
            q_n[:, hs], keys, (((1,), (1,)), ((), ())), preferred_element_type=jnp.float32
        ) * np.float32(1.0 / math.sqrt(HEAD))
        scores = jnp.where(causal, scores, -1e30)
        top = jnp.max(scores, axis=1, keepdims=True)
        expd = jnp.exp(scores - top)
        probs[h] = (expd / jnp.sum(expd, axis=1, keepdims=True)).astype(jnp.bfloat16)
    v_copy.wait_recv()
    values = far_kv[1]
    for h in range(QH):
        hs = pl.ds(h * HEAD, HEAD)
        attn = jnp.dot(probs[h], values, preferred_element_type=jnp.float32)
        passed[0, :, hs] = (far_x[:, hs].astype(jnp.float32) + attn).astype(jnp.bfloat16)

    for c in (head_copy, inv_copy, k_copy, v_copy):
        c.wait_send()

    for k in range(depth):

        @pl.when(z == k)
        def _():
            sent = slots.at[pl.ds(0, group - 1 + group * k)]
            pltpu.make_async_copy(sent, sent, part_send).wait()

    for zz in range(1, depth):

        @pl.when(z < zz)
        def _():
            lift(zz).wait_send()

    def sent(n, sem):
        span = w.at[0, pl.ds(0, n * chunk)]
        pltpu.make_async_copy(span, span, sem).wait()

    n, t = len(units), len(turns)

    @pl.when(inner)
    def _():
        sent(3 * (n + t), p_send)
        sent(2 * (n + t), q_send)

    @pl.when(outer)
    def _():
        sent(n + t, p_send)

    sent(n + 3 * len(straight), y_send)
    sent(8 * n, c_send)


def write_out(*refs):
    half = (len(refs) - 1) // 2
    sems = refs[-1]
    copies = [
        pltpu.make_async_copy(refs[i], refs[half + i], sems.at[i]) for i in range(half)
    ]
    for c in copies:
        c.start()
    for c in copies:
        c.wait()


def on_device(n_dp, n_pipe, master, grads, first_moment, second_moment, tokens):
    _, blocks, rows, cols = master.shape
    _, seq, dim = tokens.shape
    total = n_dp * n_pipe
    count = grads.size * total
    pieces = max(1, rows // PIECE)
    f32, bf16 = jnp.float32, jnp.bfloat16
    hbm = pl.BlockSpec(memory_space=pltpu.HBM)
    vmem = pl.BlockSpec(memory_space=pltpu.VMEM)
    dma = pltpu.SemaphoreType.DMA
    shapes = (
        *[jax.ShapeDtypeStruct(master.shape, f32)] * 3,
        jax.ShapeDtypeStruct((1, seq, WIDTH), bf16),
    )
    master, grads, first_moment, second_moment, tokens = (
        pltpu.with_memory_space_constraint(v, pltpu.HBM)
        for v in (master, grads, first_moment, second_moment, tokens)
    )
    depth = n_dp // 4
    if depth == 4 and rows % CHUNK == 0 and cols == 2 * HEAD:
        turned = PAIR_TURNED if rows // CHUNK > PAIR_TURNED else 0
        body = functools.partial(paired, n_dp, n_pipe, count, turned)
        scratch = [
            *[pltpu.VMEM((blocks, rows, cols), f32)] * 4,
            pltpu.VMEM((seq, dim), bf16),
            pltpu.VMEM((seq, dim), bf16),
            pltpu.VMEM((2, n_dp * rows, HEAD), bf16),
            pltpu.VMEM((seq, cols), f32),
            pltpu.VMEM((1, 128), f32),
            pltpu.VMEM((total, 1, 128), f32),
            pltpu.VMEM((depth, 1, 128), f32),
            pltpu.VMEM((seq, 128), f32),
            pltpu.VMEM((2, seq, HEAD), bf16),
            pltpu.VMEM((seq, WIDTH), bf16),
            pltpu.VMEM((QH, seq, seq), bf16),
            pltpu.VMEM((seq, WIDTH), bf16),
            pltpu.VMEM((seq, 128), f32),
            pltpu.VMEM((2, seq, HEAD), bf16),
            dma((8,)),
            dma,
            dma((depth,)),
            dma((depth,)),
            dma((depth,)),
            pltpu.SemaphoreType.REGULAR((depth,)),
            dma,
            dma,
            dma,
            dma,
            dma((2, n_dp, rows // CHUNK)),
            dma((4,)),
            dma((4,)),
        ]
    else:
        body = functools.partial(kernel, n_dp, n_pipe, count, TURNED if pieces > TURNED else 0)
        scratch = [
            pltpu.VMEM((blocks, rows, cols), f32),
            pltpu.VMEM((blocks, rows, cols), f32),
            pltpu.VMEM((blocks, rows, cols), f32),
            pltpu.VMEM((blocks, rows, cols), f32),
            pltpu.VMEM((seq, dim), bf16),
            pltpu.VMEM((seq, dim), bf16),
            pltpu.VMEM((n_dp * rows, cols), bf16),
            pltpu.VMEM((seq, cols), f32),
            pltpu.VMEM((1, 128), f32),
            pltpu.VMEM((total, 1, 128), f32),
            pltpu.VMEM((seq, 128), f32),
            pltpu.VMEM((seq, cols), bf16),
            pltpu.VMEM((seq, WIDTH), bf16),
            pltpu.VMEM((seq, WIDTH), bf16),
            pltpu.VMEM((seq, 128), f32),
            pltpu.VMEM((seq, cols), bf16),
            dma((8,)),
            dma,
            dma,
            dma,
            dma((2, 2, depth, pieces)),
            dma((depth, pieces)),
            dma((n_dp // 2, pieces)),
            dma((n_dp, pieces)),
            dma((3,)),
            dma((3,)),
        ]
    results = pl.pallas_call(
        body,
        out_shape=tuple(pltpu.VMEM(v.shape, v.dtype) for v in shapes),
        in_specs=[hbm] * 5,
        out_specs=(vmem,) * 4,
        scratch_shapes=scratch,
        compiler_params=pltpu.CompilerParams(
            collective_id=0, has_side_effects=True, vmem_limit_bytes=48 * 1024 * 1024
        ),
        name="section",
    )(master, grads, first_moment, second_moment, tokens)
    return pl.pallas_call(
        write_out,
        out_shape=shapes,
        in_specs=[vmem] * 4,
        out_specs=(hbm,) * 4,
        scratch_shapes=[dma((4,))],
        compiler_params=pltpu.CompilerParams(vmem_limit_bytes=1024 * 1024),
        name="write_out",
    )(*results)


def solution(mesh):
    split = P("pipe", None, "dp", None)
    rows = P("pipe", "dp", None)
    return jax.shard_map(
        functools.partial(on_device, mesh.shape["dp"], mesh.shape["pipe"]),
        mesh=mesh,
        in_specs=(split, split, split, split, rows),
        out_specs=(split, split, split, rows),
        check_vma=False,
    )
```

```python
import functools
import math

import jax
import jax.numpy as jnp
import numpy as np
from jax import lax
from jax.experimental import pallas as pl
from jax.experimental.pallas import tpu as pltpu
from jax.sharding import PartitionSpec as P

HEAD = 128
QH = 8
PIECE = 256
TURNED = 0
CHUNK = 128
PAIR_TURNED = 1
STEP = 10
WIDTH = QH * HEAD
MESH = pl.DeviceIdType.MESH


def adam(master, grads, first_moment, second_moment, clip):
    scaled = clip * grads
    new_first = 0.9 * first_moment + 0.1 * scaled
    new_second = 0.95 * second_moment + 0.05 * scaled * scaled
    step_mean = new_first / (1.0 - 0.9**STEP)
    step_var = new_second / (1.0 - 0.95**STEP)
    new_master = master - 0.003 * step_mean / (jnp.sqrt(step_var) + 1e-08)
    return new_master, new_first, new_second


def kernel(
    n_dp, n_pipe, count, turned,
    master, grads, first, second, tokens,
    new_master, new_first, new_second, passed,
    g_v, m_v, f_v, s_v, x_v, n_v, w, acc, part, slots, inv, kv, q_n,
    far_x, far_inv, far_kv,
    load_sem, own_sem, part_send, part_recv, z_send, y_send, c_send, w_recv,
    far_send, far_recv,
):
    me = lax.axis_index("dp")
    sec = lax.axis_index("pipe")
    total = n_dp * n_pipe
    lines, cores = 2, 2
    depth = n_dp // (lines * cores)
    core = lax.rem(me, cores)
    line = lax.rem(lax.div(me, cores), lines)
    z = lax.div(me, lines * cores)
    mine = (z, line, core)
    rows = g_v.shape[1]
    pieces = w_recv.shape[1]
    piece = rows // pieces
    dim = x_v.shape[1]
    seq = x_v.shape[0]

    def at(zz, yy, cc):
        return (zz * lines + yy) * cores + cc

    blocks = g_v.shape[0]
    states = ((master, m_v), (first, f_v), (second, s_v))
    loads = [
        pltpu.make_async_copy(grads.at[0], g_v, load_sem.at[0]),
        *[
            pltpu.make_async_copy(src.at[0, 0], dst.at[0], load_sem.at[1 + i])
            for i, (src, dst) in enumerate(states)
        ],
        pltpu.make_async_copy(tokens.at[0], x_v, load_sem.at[4]),
        *[
            pltpu.make_async_copy(
                src.at[0, pl.ds(1, blocks - 1)], dst.at[pl.ds(1, blocks - 1)], load_sem.at[5 + i]
            )
            for i, (src, dst) in enumerate(states)
        ],
    ]
    loads[0].start()

    flat = sec * n_dp + me

    def peer(k):
        other = lax.rem(flat + k, total)
        return {"dp": lax.rem(other, n_dp), "pipe": lax.div(other, n_dp)}

    barrier = pltpu.get_barrier_semaphore()

    @pl.loop(1, total)
    def _(k):
        pl.semaphore_signal(barrier, inc=1, device_id=peer(k), device_id_type=MESH)

    for load in loads[1:]:
        load.start()

    loads[0].wait()
    cols = g_v.shape[2]
    local = jnp.zeros((8, cols), jnp.float32)
    for b in range(blocks):
        g = g_v[b]
        local = local + jnp.sum((g * g).reshape(rows // 8, 8, cols), axis=0)
    lanes = local[:, :128]
    for i in range(1, cols // 128):
        lanes = lanes + local[:, i * 128 : (i + 1) * 128]
    part[...] = jnp.sum(lanes, axis=0, keepdims=True)

    pl.semaphore_wait(barrier, total - 1)

    own = pltpu.make_async_copy(part, slots.at[flat], part_recv)
    own.start()

    @pl.loop(1, total)
    def _(k):
        pltpu.make_async_remote_copy(
            src_ref=part, dst_ref=slots.at[flat], send_sem=part_send, recv_sem=part_recv,
            device_id=peer(k), device_id_type=MESH,
        ).start()

    after = lax.rem(sec + 1, n_pipe)

    def to_next(src, dst, i):
        return pltpu.make_async_remote_copy(
            src_ref=src, dst_ref=dst, send_sem=far_send.at[i], recv_sem=far_recv.at[i],
            device_id={"dp": me, "pipe": after}, device_id_type=MESH,
        )

    head_copy = to_next(tokens.at[0, :, pl.ds(0, WIDTH)], far_x, 0)

    loads[4].wait()
    step = 512

    def squares(i, carry):
        for j in range(step // 128):
            x = x_v[:, pl.ds(pl.multiple_of(i * step + j * 128, 128), 128)].astype(jnp.float32)
            carry = carry + x * x
        return carry

    sq = lax.fori_loop(0, dim // step, squares, jnp.zeros((seq, 128), jnp.float32))
    mean_sq = jnp.sum(sq, axis=1, keepdims=True) / dim
    inv[...] = jnp.broadcast_to(lax.rsqrt(mean_sq + 1e-06), (seq, 128))
    inv_copy = to_next(inv, far_inv, 1)
    inv_copy.start()

    @pl.loop(0, dim // step)
    def _(i):
        scale = inv[...]
        for j in range(step // 128):
            at_cols = pl.ds(pl.multiple_of(i * step + j * 128, 128), 128)
            n_v[:, at_cols] = (x_v[:, at_cols].astype(jnp.float32) * scale).astype(jnp.bfloat16)

    for load in loads[1:4]:
        load.wait()
    acc[...] = jnp.zeros_like(acc)

    pltpu.make_async_copy(slots, slots, part_recv).wait()
    summed = jnp.sum(slots[...], axis=0)
    square_sum = jnp.sum(summed, axis=1, keepdims=True)
    root = np.float32(0.5) * np.sqrt(np.float32(count))
    clip = jnp.minimum(1.0, root / jnp.sqrt(square_sum + 1e-06))

    def span(b, ch):
        return pl.ds(pl.multiple_of(at(*b) * rows + ch * piece, piece), piece)

    def send(b, ch, dst, sem):
        return pltpu.make_async_remote_copy(
            src_ref=w.at[span(b, ch)], dst_ref=w.at[span(b, ch)],
            send_sem=sem, recv_sem=w_recv.at[at(*b), ch],
            device_id={"dp": dst, "pipe": sec}, device_id_type=MESH,
        )

    def chip(b):
        return b[0]

    def up(b, ch, other=0):
        return send(b, ch, at(z + 1, line, core), z_send.at[0, other, chip(b), ch])

    def down(b, ch, other=0):
        return send(b, ch, at(z - 1, line, core), z_send.at[1, other, chip(b), ch])

    def across(b, ch):
        return send(b, ch, at(z, 1 - line, core), y_send.at[chip(b), ch])

    def beside(b, ch):
        return send(b, ch, at(z, line, 1 - core), c_send.at[b[0] * lines + b[1], ch])

    def arrived(b, ch):
        send(b, ch, me, c_send.at[0, 0]).wait_recv()

    def both_ways(b, ch, other=0):
        @pl.when(z < depth - 1)
        def _():
            up(b, ch, other).start()

        @pl.when(z > 0)
        def _():
            down(b, ch, other).start()

    whole_blocks = rows % 128 == 0

    def multiply(b):
        if whole_blocks:
            at_rows = pl.ds(pl.multiple_of(at(*b) * rows, rows), rows)
            acc[...] += jnp.dot(n_v[:, at_rows], w[at_rows, :], preferred_element_type=jnp.float32)

    def update(b, r):
        results = adam(m_v[b, r, :], g_v[b, r, :], f_v[b, r, :], s_v[b, r, :], clip)
        for ref, result in zip((new_master, new_first, new_second), results):
            ref[0, b, r, :] = result
        return results[0]

    def multiply_piece(b, ch):
        if whole_blocks:
            at_rows = span(b, ch)
            acc[...] += jnp.dot(n_v[:, at_rows], w[at_rows, :], preferred_element_type=jnp.float32)

    for ch in range(pieces):
        w[span(mine, ch), :] = update(0, pl.ds(ch * piece, piece)).astype(jnp.bfloat16)
        both_ways(mine, ch)
        across(mine, ch).start()
        beside(mine, ch).start()

    head_copy.start()
    multiply(mine)

    for ch in range(turned):
        b = (z, 1 - line, core)
        arrived(b, ch)
        both_ways(b, ch, 1)
        beside(b, ch).start()

    for t in range(depth):
        far = t + 1
        if far < depth:
            for other in (0, 1):
                for ch in range(pieces if other == 0 else turned):

                    def along(zz, onward, end):
                        b = (zz, (line, 1 - line)[other], core)
                        arrived(b, ch)

                        @pl.when(end)
                        def _():
                            onward(b, ch, other).start()

                        if other == 0 and ch >= turned:
                            across(b, ch).start()
                        beside(b, ch).start()

                    @pl.when(z - far >= 0)
                    def _():
                        along(z - far, up, z < depth - 1)

                    @pl.when(z + far < depth)
                    def _():
                        along(z + far, down, z > 0)

        def at_distance(visit):
            if t == 0:
                visit(z)
            else:

                @pl.when(z - t >= 0)
                def _():
                    visit(z - t)

                @pl.when(z + t < depth)
                def _():
                    visit(z + t)

        last = t == depth - 1
        if last:

            def use_own(zz):
                multiply((zz, line, core))
                b = (zz, line, 1 - core)
                for ch in range(pieces):
                    arrived(b, ch)
                multiply(b)

            at_distance(use_own)
        for ch in range(turned, pieces):

            def pass_on(zz):
                b = (zz, 1 - line, core)
                arrived(b, ch)
                beside(b, ch).start()
                if last:
                    multiply_piece(b, ch)

            at_distance(pass_on)

        def use(zz):
            if last:
                for ch in range(turned):
                    multiply_piece((zz, 1 - line, core), ch)
                b = (zz, 1 - line, 1 - core)
                for ch in range(pieces):
                    arrived(b, ch)
                    multiply_piece(b, ch)
                return
            if t > 0:
                multiply((zz, line, core))
            multiply((zz, 1 - line, core))
            for yy in (line, 1 - line):
                b = (zz, yy, 1 - core)
                for ch in range(pieces):
                    arrived(b, ch)
                multiply(b)

        if t == 0:
            for load in loads[5:]:
                load.wait()
            for b in range(1, blocks):
                for ch in range(pieces):
                    update(b, pl.ds(ch * piece, piece))
        if t == min(2, depth - 1):
            head_copy.wait_recv()
            inv_copy.wait_recv()
            for h in range(QH):
                hs = pl.ds(h * HEAD, HEAD)
                q_n[:, hs] = (far_x[:, hs].astype(jnp.float32) * far_inv[...]).astype(jnp.bfloat16)
        at_distance(use)

    if whole_blocks:
        projected = acc[...]
    else:

        def run(i, carry):
            d = pl.ds(pl.multiple_of(i * step, step), step)
            return carry + jnp.dot(n_v[:, d], w[d, :], preferred_element_type=jnp.float32)

        projected = lax.fori_loop(0, dim // step, run, acc[...])
    kv[...] = projected.astype(jnp.bfloat16)
    kv_copy = to_next(kv, far_kv, 2)
    kv_copy.start()
    row = lax.broadcasted_iota(jnp.int32, (seq, seq), 0)
    col = lax.broadcasted_iota(jnp.int32, (seq, seq), 1)
    causal = row >= col
    kv_copy.wait_recv()
    keys = far_kv[:, :HEAD]
    values = far_kv[:, HEAD:]
    for h in range(QH):
        hs = pl.ds(h * HEAD, HEAD)
        scores = lax.dot_general(
            q_n[:, hs], keys, (((1,), (1,)), ((), ())), preferred_element_type=jnp.float32
        ) * np.float32(1.0 / math.sqrt(HEAD))
        scores = jnp.where(causal, scores, -1e30)
        top = jnp.max(scores, axis=1, keepdims=True)
        expd = jnp.exp(scores - top)
        probs = (expd / jnp.sum(expd, axis=1, keepdims=True)).astype(jnp.bfloat16)
        attn = jnp.dot(probs, values, preferred_element_type=jnp.float32)
        passed[0, :, hs] = (far_x[:, hs].astype(jnp.float32) + attn).astype(jnp.bfloat16)

    for c in (head_copy, inv_copy, kv_copy):
        c.wait_send()
    pltpu.make_async_copy(
        slots.at[pl.ds(0, total - 1)], slots.at[pl.ds(0, total - 1)], part_send
    ).wait()
    for ch in range(pieces):
        for zz in range(depth):
            for other in range(2 if ch < turned else 1):
                b = (zz, (line, 1 - line)[other], core)

                @pl.when(jnp.logical_and(zz <= z, z < depth - 1))
                def _():
                    up(b, ch, other).wait_send()

                @pl.when(jnp.logical_and(zz >= z, z > 0))
                def _():
                    down(b, ch, other).wait_send()

            b = (zz, line, core)
            if ch >= turned:
                across(b, ch).wait_send()
            else:

                @pl.when(zz == z)
                def _():
                    across(b, ch).wait_send()

            for yy in range(lines):
                beside((zz, yy, core), ch).wait_send()


def paired(
    n_dp, n_pipe, count, turned,
    master, grads, first, second, tokens,
    new_master, new_first, new_second, passed,
    g_v, m_v, f_v, s_v, x_v, n_v, w, acc, part, slots, sums, inv, kv, q_n, probs,
    far_x, far_inv, far_kv,
    load_sem, part_send, part_recv, sum_send, sum_recv, ready, p_send, q_send, y_send, c_send,
    z_recv, y_recv, c_recv, far_send, far_recv,
):
    me = lax.axis_index("dp")
    sec = lax.axis_index("pipe")
    lines, cores, depth = 2, 2, 4
    group = n_pipe * lines * cores
    core = lax.rem(me, cores)
    line = lax.rem(lax.div(me, cores), lines)
    z = lax.div(me, lines * cores)
    seat = sec * lines * cores + lax.rem(me, lines * cores)
    upper = lax.div(z, 2)
    inner = jnp.logical_or(z == 1, z == 2)
    outer = jnp.logical_not(inner)
    planes = (z, 1 - z + 4 * upper, 2 - upper, 3 - 3 * upper)
    blocks, rows, cols = g_v.shape
    seq, dim = x_v.shape
    chunk = CHUNK
    chunks = rows // chunk
    units = [(h, c) for h in range(2) for c in range(chunks)]
    straight = [u for u in units if u[0] == 0 or u[1] >= turned]
    turns = [(1, c) for c in range(turned)]

    def at(zz, yy, cc):
        return (zz * lines + yy) * cores + cc

    def device(zz, r):
        return {"dp": zz * lines * cores + lax.rem(r, lines * cores), "pipe": lax.div(r, lines * cores)}

    states = ((master, m_v), (first, f_v), (second, s_v))
    loads = [
        pltpu.make_async_copy(grads.at[0], g_v, load_sem.at[0]),
        *[
            pltpu.make_async_copy(src.at[0, 0], dst.at[0], load_sem.at[1 + i])
            for i, (src, dst) in enumerate(states)
        ],
        pltpu.make_async_copy(tokens.at[0], x_v, load_sem.at[4]),
        *[
            pltpu.make_async_copy(
                src.at[0, pl.ds(1, blocks - 1)], dst.at[pl.ds(1, blocks - 1)], load_sem.at[5 + i]
            )
            for i, (src, dst) in enumerate(states)
        ],
    ]
    loads[0].start()
    barrier = pltpu.get_barrier_semaphore()

    @pl.loop(1, group)
    def _(k):
        pl.semaphore_signal(
            barrier, inc=1, device_id=device(z, lax.rem(seat + k, group)), device_id_type=MESH
        )

    @pl.loop(0, group * (depth - 1 - z))
    def _(k):
        pl.semaphore_signal(
            barrier, inc=1, device_id=device(z + 1 + lax.div(k, group), lax.rem(k, group)),
            device_id_type=MESH,
        )

    loads[4].start()
    for load in loads[1:4] + loads[5:]:
        load.start()

    for k in range(depth):

        @pl.when(z == k)
        def _():
            pl.semaphore_wait(barrier, group - 1 + group * k)

    @pl.loop(0, z)
    def _(zz):
        pl.semaphore_signal(
            ready.at[z], inc=1, device_id=device(zz, seat), device_id_type=MESH
        )

    loads[0].wait()
    local = jnp.zeros((8, cols), jnp.float32)
    for b in range(blocks):
        g = g_v[b]
        local = local + jnp.sum((g * g).reshape(rows // 8, 8, cols), axis=0)
    lanes = local[:, :128]
    for i in range(1, cols // 128):
        lanes = lanes + local[:, i * 128 : (i + 1) * 128]
    part[...] = jnp.sum(lanes, axis=0, keepdims=True)


    def give(zz, r):
        return pltpu.make_async_remote_copy(
            src_ref=part, dst_ref=slots.at[z * group + seat], send_sem=part_send,
            recv_sem=part_recv.at[z], device_id=device(zz, r), device_id_type=MESH,
        )

    own = pltpu.make_async_copy(part, slots.at[z * group + seat], part_recv.at[z])
    own.start()

    @pl.loop(0, group * z)
    def _(k):
        give(lax.div(k, group), lax.rem(k, group)).start()

    @pl.loop(1, group)
    def _(k):
        give(z, lax.rem(seat + k, group)).start()

    after = lax.rem(sec + 1, n_pipe)

    def to_next(src, dst, i):
        return pltpu.make_async_remote_copy(
            src_ref=src, dst_ref=dst, send_sem=far_send.at[i], recv_sem=far_recv.at[i],
            device_id={"dp": me, "pipe": after}, device_id_type=MESH,
        )

    head_copy = to_next(tokens.at[0, :, pl.ds(0, WIDTH)], far_x, 0)

    loads[4].wait()
    step = 512

    def squares(i, carry):
        for j in range(step // 128):
            x = x_v[:, pl.ds(pl.multiple_of(i * step + j * 128, 128), 128)].astype(jnp.float32)
            carry = carry + x * x
        return carry

    sq = lax.fori_loop(0, dim // step, squares, jnp.zeros((seq, 128), jnp.float32))
    mean_sq = jnp.sum(sq, axis=1, keepdims=True) / dim
    inv[...] = jnp.broadcast_to(lax.rsqrt(mean_sq + 1e-06), (seq, 128))
    inv_copy = to_next(inv, far_inv, 1)


    @pl.loop(0, dim // step)
    def _(i):
        scale = inv[...]
        for j in range(step // 128):
            at_cols = pl.ds(pl.multiple_of(i * step + j * 128, 128), 128)
            n_v[:, at_cols] = (x_v[:, at_cols].astype(jnp.float32) * scale).astype(jnp.bfloat16)

    acc[...] = jnp.zeros_like(acc)

    def plane_slots(zz):
        return slots.at[pl.ds(zz * group, group)]

    def plane_wait(zz):
        pltpu.make_async_copy(plane_slots(zz), plane_slots(zz), part_recv.at[zz]).wait()

    plane_wait(z)
    sums[z] = jnp.sum(plane_slots(z)[...], axis=0)

    def lift(zz):
        return pltpu.make_async_remote_copy(
            src_ref=sums.at[z], dst_ref=sums.at[z], send_sem=sum_send.at[zz],
            recv_sem=sum_recv.at[z], device_id=device(zz, seat), device_id_type=MESH,
        )

    for zz in range(1, depth):

        @pl.when(z < zz)
        def _():
            pl.semaphore_wait(ready.at[zz], 1)
            lift(zz).start()

    for load in loads[1:4]:
        load.wait()
    for zz in range(depth):

        @pl.when(zz > z)
        def _():
            plane_wait(zz)
            sums[zz] = jnp.sum(plane_slots(zz)[...], axis=0)

        @pl.when(zz < z)
        def _():
            pltpu.make_async_copy(sums.at[zz], sums.at[zz], sum_recv.at[zz]).wait()

    square_sum = jnp.sum(jnp.sum(sums[...], axis=0), axis=1, keepdims=True)
    root = np.float32(0.5) * np.sqrt(np.float32(count))
    clip = jnp.minimum(1.0, root / jnp.sqrt(square_sum + 1e-06))

    def span(b, u):
        h, low, size = u
        return w.at[h, pl.ds(pl.multiple_of(at(*b) * rows + low, chunk), size)]

    def send(b, u, dst, sem, recv):
        pltpu.make_async_remote_copy(
            src_ref=span(b, u), dst_ref=span(b, u), send_sem=sem, recv_sem=recv,
            device_id={"dp": dst, "pipe": sec}, device_id_type=MESH,
        ).start()

    def wait(b, u, sem):
        pltpu.make_async_copy(span(b, u), span(b, u), sem).wait()

    def one(u):
        return (u[0], u[1] * chunk, chunk)

    low = turned * chunk
    keys_of, values_of, turned_of = (0, 0, rows), (1, low, rows - low), (1, 0, low)
    groups = [keys_of, values_of] + ([turned_of] if turned else [])
    beyond = jnp.where(z == 1, 2, 1)

    def z_sem(s, u):
        return z_recv.at[planes[s], u[0], u[1]]

    def y_sem(s, g):
        return y_recv.at[planes[s], groups.index(g)]

    def to_pair(s, u):
        send(here(s), one(u), at(planes[1], line, core), p_send, z_sem(s, u))

    def to_beyond(s, u):
        send(here(s), one(u), at(beyond, line, core), q_send, z_sem(s, u))

    def turn_to_pair(s):
        send(there(s), turned_of, at(planes[1], line, core), p_send, y_sem(s, turned_of))

    def turn_to_beyond(s):
        send(there(s), turned_of, at(beyond, line, core), q_send, y_sem(s, turned_of))

    def across(s, u):
        g = keys_of if u[0] == 0 else turned_of if u in turns else values_of
        send(here(s), one(u), at(z, 1 - line, core), y_send, y_sem(s, g))

    def beside(s, u):
        send(here(s), one(u), at(z, line, 1 - core), c_send, c_recv.at[planes[s], u[0]])

    def group_beside(s, g):
        send(there(s), g, at(z, line, 1 - core), c_send, c_recv.at[planes[s], 2 + groups.index(g)])

    def arrived(s, u):
        wait(here(s), one(u), z_sem(s, u))

    def group_arrived(s, g):
        wait(there(s), g, y_sem(s, g))

    def pass_groups(s, some):
        for g in some:
            group_arrived(s, g)
            group_beside(s, g)

    def side(s, h):
        wait((planes[s], line, 1 - core), (h, 0, rows), c_recv.at[planes[s], h])

    def side_group(s, g):
        wait((planes[s], 1 - line, 1 - core), g, c_recv.at[planes[s], 2 + groups.index(g)])

    def here(s):
        return (planes[s], line, core)

    def there(s):
        return (planes[s], 1 - line, core)

    def update(b, r, hs):
        results = adam(m_v[b, r, hs], g_v[b, r, hs], f_v[b, r, hs], s_v[b, r, hs], clip)
        for ref, result in zip((new_master, new_first, new_second), results):
            ref[0, b, r, hs] = result
        return results[0]

    halves = (slice(0, HEAD), slice(HEAD, 2 * HEAD))

    def product(h, s, yy, cc, low, size):
        d = pl.ds(pl.multiple_of(at(planes[s], yy, cc) * rows + low, 128), size)
        return jnp.dot(n_v[:, d], w[h, d, :], preferred_element_type=jnp.float32)

    def product_line(s, yy, h=None):
        d = pl.ds(pl.multiple_of(at(planes[s], yy, 0) * rows, rows), cores * rows)
        own = w[h, d, :] if h is not None else jnp.concatenate([w[0, d, :], w[1, d, :]], axis=1)
        return jnp.dot(n_v[:, d], own, preferred_element_type=jnp.float32)

    def straight_values(s):
        return product(1, s, 1 - line, 0, low, rows - low) + product(1, s, 1 - line, 1, low, rows - low)

    def multiply(s):
        acc[...] += product_line(s, line)
        acc[:, halves[0]] += product_line(s, 1 - line, 0)
        acc[:, halves[1]] += straight_values(s)

    for h, c in units:
        r = pl.ds(c * chunk, chunk)
        w[h, pl.ds(pl.multiple_of(me * rows + c * chunk, chunk), chunk), :] = update(
            0, r, slice(h * HEAD, (h + 1) * HEAD)
        ).astype(jnp.bfloat16)
        u = (h, c)
        to_pair(0, u)

        @pl.when(inner)
        def _():
            to_beyond(0, u)

        across(0, u)
        beside(0, u)

    head_copy.start()
    inv_copy.start()
    for load in loads[5:]:
        load.wait()
    for b in range(1, blocks):
        for c in range(chunks):
            for h in range(2):
                update(b, pl.ds(c * chunk, chunk), slice(h * HEAD, (h + 1) * HEAD))

    for u in units:
        arrived(1, u)

        @pl.when(inner)
        def _():
            to_beyond(1, u)
            arrived(2, u)
            to_pair(2, u)
            beside(2, u)

        if u in straight:
            across(1, u)
        beside(1, u)

    @pl.when(inner)
    def _():
        for u in straight:
            across(2, u)

    pass_groups(0, groups)
    if turned:

        @pl.when(inner)
        def _():
            turn_to_beyond(0)

        @pl.when(outer)
        def _():
            turn_to_pair(0)

    for h in range(2):
        side(0, h)
    for g in groups:
        side_group(0, g)
    acc[...] += product_line(0, line) + product_line(0, 1 - line)

    for u in units:

        @pl.when(inner)
        def _():
            arrived(3, u)
            to_pair(3, u)
            across(3, u) if u in straight else None
            beside(3, u)

        @pl.when(outer)
        def _():
            arrived(2, u)
            across(2, u) if u in straight else None
            beside(2, u)

    pass_groups(1, groups[:2])
    if turned:

        @pl.when(inner)
        def _():
            group_arrived(1, turned_of)
            turn_to_beyond(1)
            group_beside(1, turned_of)
            turn_to_pair(0)
            for s in (2, 3):
                group_arrived(s, turned_of)
                turn_to_pair(s)
                group_beside(s, turned_of)

    for h in range(2):
        side(1, h)
        side_group(1, groups[h])
    multiply(1)
    head_copy.wait_recv()
    inv_copy.wait_recv()
    for h in range(QH):
        hs = pl.ds(h * HEAD, HEAD)
        q_n[:, hs] = (far_x[:, hs].astype(jnp.float32) * far_inv[...]).astype(jnp.bfloat16)


    @pl.when(outer)
    def _():
        for u in units:
            arrived(3, u)
            across(3, u) if u in straight else None
            beside(3, u)

    pass_groups(2, groups[:2])
    for h in range(2):
        side(2, h)
        side_group(2, groups[h])
    multiply(2)

    side(3, 0)
    acc[:, halves[0]] += product_line(3, line, 0)
    pass_groups(3, [keys_of])
    if turned:

        @pl.when(outer)
        def _():
            for s in (1, 2, 3):
                pass_groups(s, [turned_of])

    side_group(3, keys_of)
    kv[0] = (acc[:, halves[0]] + product_line(3, 1 - line, 0)).astype(jnp.bfloat16)
    k_copy = to_next(kv.at[0], far_kv.at[0], 2)
    k_copy.start()
    side(3, 1)
    acc[:, halves[1]] += product_line(3, line, 1)
    pass_groups(3, [values_of])
    if turned:
        for s in (1, 2, 3):
            side_group(s, turned_of)
        acc[:, halves[1]] += sum(
            product(1, s, 1 - line, cc, 0, low) for s in (1, 2, 3) for cc in range(cores)
        )
    side_group(3, values_of)
    kv[1] = (acc[:, halves[1]] + straight_values(3)).astype(jnp.bfloat16)
    v_copy = to_next(kv.at[1], far_kv.at[1], 3)
    v_copy.start()
    row = lax.broadcasted_iota(jnp.int32, (seq, seq), 0)
    col = lax.broadcasted_iota(jnp.int32, (seq, seq), 1)
    causal = row >= col
    k_copy.wait_recv()
    keys = far_kv[0]
    for h in range(QH):
        hs = pl.ds(h * HEAD, HEAD)
        scores = lax.dot_general(
            q_n[:, hs], keys, (((1,), (1,)), ((), ())), preferred_element_type=jnp.float32
        ) * np.float32(1.0 / math.sqrt(HEAD))
        scores = jnp.where(causal, scores, -1e30)
        top = jnp.max(scores, axis=1, keepdims=True)
        expd = jnp.exp(scores - top)
        probs[h] = (expd / jnp.sum(expd, axis=1, keepdims=True)).astype(jnp.bfloat16)
    v_copy.wait_recv()
    values = far_kv[1]
    for h in range(QH):
        hs = pl.ds(h * HEAD, HEAD)
        attn = jnp.dot(probs[h], values, preferred_element_type=jnp.float32)
        passed[0, :, hs] = (far_x[:, hs].astype(jnp.float32) + attn).astype(jnp.bfloat16)

    for c in (head_copy, inv_copy, k_copy, v_copy):
        c.wait_send()

    for k in range(depth):

        @pl.when(z == k)
        def _():
            sent = slots.at[pl.ds(0, group - 1 + group * k)]
            pltpu.make_async_copy(sent, sent, part_send).wait()

    for zz in range(1, depth):

        @pl.when(z < zz)
        def _():
            lift(zz).wait_send()

    def sent(n, sem):
        whole = w.at[0, pl.ds(0, n * chunk)]
        pltpu.make_async_copy(whole, whole, sem).wait()

    n, t = len(units), len(turns)

    @pl.when(inner)
    def _():
        sent(3 * (n + t), p_send)
        sent(2 * (n + t), q_send)

    @pl.when(outer)
    def _():
        sent(n + t, p_send)

    sent(n + 3 * len(straight), y_send)
    sent(8 * n, c_send)


def write_out(*refs):
    half = (len(refs) - 1) // 2
    sems = refs[-1]
    copies = [
        pltpu.make_async_copy(refs[i], refs[half + i], sems.at[i]) for i in range(half)
    ]
    for c in copies:
        c.start()
    for c in copies:
        c.wait()


def on_device(n_dp, n_pipe, master, grads, first_moment, second_moment, tokens):
    _, blocks, rows, cols = master.shape
    _, seq, dim = tokens.shape
    total = n_dp * n_pipe
    count = grads.size * total
    pieces = max(1, rows // PIECE)
    f32, bf16 = jnp.float32, jnp.bfloat16
    hbm = pl.BlockSpec(memory_space=pltpu.HBM)
    vmem = pl.BlockSpec(memory_space=pltpu.VMEM)
    dma = pltpu.SemaphoreType.DMA
    shapes = (
        *[jax.ShapeDtypeStruct(master.shape, f32)] * 3,
        jax.ShapeDtypeStruct((1, seq, WIDTH), bf16),
    )
    master, grads, first_moment, second_moment, tokens = (
        pltpu.with_memory_space_constraint(v, pltpu.HBM)
        for v in (master, grads, first_moment, second_moment, tokens)
    )
    depth = n_dp // 4
    if depth == 4 and rows % CHUNK == 0 and cols == 2 * HEAD:
        turned = PAIR_TURNED if rows // CHUNK > PAIR_TURNED else 0
        body = functools.partial(paired, n_dp, n_pipe, count, turned)
        scratch = [
            *[pltpu.VMEM((blocks, rows, cols), f32)] * 4,
            pltpu.VMEM((seq, dim), bf16),
            pltpu.VMEM((seq, dim), bf16),
            pltpu.VMEM((2, n_dp * rows, HEAD), bf16),
            pltpu.VMEM((seq, cols), f32),
            pltpu.VMEM((1, 128), f32),
            pltpu.VMEM((total, 1, 128), f32),
            pltpu.VMEM((depth, 1, 128), f32),
            pltpu.VMEM((seq, 128), f32),
            pltpu.VMEM((2, seq, HEAD), bf16),
            pltpu.VMEM((seq, WIDTH), bf16),
            pltpu.VMEM((QH, seq, seq), bf16),
            pltpu.VMEM((seq, WIDTH), bf16),
            pltpu.VMEM((seq, 128), f32),
            pltpu.VMEM((2, seq, HEAD), bf16),
            dma((8,)),
            dma,
            dma((depth,)),
            dma((depth,)),
            dma((depth,)),
            pltpu.SemaphoreType.REGULAR((depth,)),
            dma,
            dma,
            dma,
            dma,
            dma((depth, 2, rows // CHUNK)),
            dma((depth, 3)),
            dma((depth, 5)),
            dma((4,)),
            dma((4,)),
        ]
    else:
        body = functools.partial(kernel, n_dp, n_pipe, count, TURNED if pieces > TURNED else 0)
        scratch = [
            pltpu.VMEM((blocks, rows, cols), f32),
            pltpu.VMEM((blocks, rows, cols), f32),
            pltpu.VMEM((blocks, rows, cols), f32),
            pltpu.VMEM((blocks, rows, cols), f32),
            pltpu.VMEM((seq, dim), bf16),
            pltpu.VMEM((seq, dim), bf16),
            pltpu.VMEM((n_dp * rows, cols), bf16),
            pltpu.VMEM((seq, cols), f32),
            pltpu.VMEM((1, 128), f32),
            pltpu.VMEM((total, 1, 128), f32),
            pltpu.VMEM((seq, 128), f32),
            pltpu.VMEM((seq, cols), bf16),
            pltpu.VMEM((seq, WIDTH), bf16),
            pltpu.VMEM((seq, WIDTH), bf16),
            pltpu.VMEM((seq, 128), f32),
            pltpu.VMEM((seq, cols), bf16),
            dma((8,)),
            dma,
            dma,
            dma,
            dma((2, 2, depth, pieces)),
            dma((depth, pieces)),
            dma((n_dp // 2, pieces)),
            dma((n_dp, pieces)),
            dma((3,)),
            dma((3,)),
        ]
    results = pl.pallas_call(
        body,
        out_shape=tuple(pltpu.VMEM(v.shape, v.dtype) for v in shapes),
        in_specs=[hbm] * 5,
        out_specs=(vmem,) * 4,
        scratch_shapes=scratch,
        compiler_params=pltpu.CompilerParams(
            collective_id=0, has_side_effects=True, vmem_limit_bytes=48 * 1024 * 1024
        ),
        name="section",
    )(master, grads, first_moment, second_moment, tokens)
    return pl.pallas_call(
        write_out,
        out_shape=shapes,
        in_specs=[vmem] * 4,
        out_specs=(hbm,) * 4,
        scratch_shapes=[dma((4,))],
        compiler_params=pltpu.CompilerParams(vmem_limit_bytes=1024 * 1024),
        name="write_out",
    )(*results)


def solution(mesh):
    split = P("pipe", None, "dp", None)
    rows = P("pipe", "dp", None)
    return jax.shard_map(
        functools.partial(on_device, mesh.shape["dp"], mesh.shape["pipe"]),
        mesh=mesh,
        in_specs=(split, split, split, split, rows),
        out_specs=(split, split, split, rows),
        check_vma=False,
    )
```
